32 devices in a mesh: seq: 8 (over z, core), head: 4 (over y, x).
Axes of the slice: x: 2, y: 2, z: 4, core: 2. Of those that a mesh axis runs over, the one named last changes fastest.
Arguments:
- queries: bfloat16 [1024, 4096], P('seq', 'head'), may hold values from -360 to 360, as said below
- keys: bfloat16 [1024, 256], P('seq', 'head'), may hold values from -6 to 6
- values: bfloat16 [1024, 256], P('seq', 'head'), may hold values from -6 to 6
- directions: bfloat16 [1024, 256], P('seq', 'head'), may hold values from -6 to 6
- beta: float32 [1024, 2], P('seq'), may hold values from 0.25 to 2
- gain: float32 [128], replicated, may hold values from 0.25 to 1.75
Outputs:
- attended: bfloat16 [1024, 4096], P('seq', 'head')
The draws below stay inside these ranges and needn't reach their ends.
Inputs may be any that keep to these rules, and one draw needn't show every extreme that they name: `queries`: queries of order one; some rows may be far larger.
All inputs are finite; a program needn't handle non-finite values.
Results may differ from the reference program's by a relative error of at most 0.04.
Values may be sent and summed in bfloat16 or wider, within the bound.
No kernel may reach another device: no remote copies, remote signals or barrier semaphores. Data moves between devices by JAX's collectives and lax.ppermute only.
A program may use at most 64 MiB of HBM per device.

```python
import jax
import jax.numpy as jnp
from jax import lax

HD = 128
GROUP_HEADS = 16
HEADS = 32
GROUPS = 2
TOK_DEV = 128
TOKENS = 1024
N_SEQ = 8


def draw_queries(key, part):
    samples = jnp.clip(jax.random.normal(key, (TOKENS, HEADS * HD), jnp.float32), -6.0, 6.0)
    return samples.astype(jnp.bfloat16)


def draw_beta(key, part):
    common = jax.random.uniform(jax.random.fold_in(key, 11), (TOKENS, GROUPS), jnp.float32, 1.95, 2.0)
    strong = jax.random.uniform(jax.random.fold_in(key, 12), (TOKENS, GROUPS), jnp.float32, 0.25, 2.0)
    picker = jax.random.randint(jax.random.fold_in(key, 13), (TOKENS, GROUPS), 0, 32)
    return jnp.where(picker == 0, strong, common).astype(jnp.float32)


def levels(rng, dims, split, least, top_value):
    def one(position, blocks):
        heights = jax.random.uniform(jax.random.fold_in(jax.random.fold_in(rng, 6), position), (blocks,), jnp.float32, least / len(split), top_value / len(split))
        return jnp.repeat(jnp.exp(heights), dims[position] // blocks).reshape((-1,) + (1,) * (len(dims) - position - 1))

    loudness = one(*split[0])
    for cut in split[1:]:
        loudness = loudness * one(*cut)
    return loudness


def bell_draw(stream_key, dims, scale, reach, cuts=(), kind=jnp.bfloat16):
    result = scale * jax.random.normal(stream_key, dims, jnp.float32)
    if cuts:
        result = result * levels(stream_key, dims, cuts, -0.22, 0.18)
    return jnp.clip(result, -reach, reach).astype(kind)


def setup_inputs(seed: int = 0) -> dict:
    key_of = jax.random.split(jax.random.key(seed), 7)
    queries = draw_queries(jax.random.fold_in(key_of[6], 71), 0)
    keys = bell_draw(key_of[1], (TOKENS, GROUPS * HD), 1.0, 6.0, ((0, 8), (1, 4)))
    values = bell_draw(key_of[2], (TOKENS, GROUPS * HD), 1.0, 6.0, ((0, 8), (1, 4)))
    directions = bell_draw(key_of[3], (TOKENS, GROUPS * HD), 1.0, 6.0, ((0, 8), (1, 4)))
    beta = draw_beta(jax.random.fold_in(key_of[6], 71), 0)
    gain = jnp.clip(1.0 + 0.15 * jax.random.normal(key_of[5], (HD,), jnp.float32), 0.25, 1.75)
    return {"queries": queries, "keys": keys, "values": values, "directions": directions, "beta": beta, "gain": gain}


exact_mode = lax.Precision.HIGHEST

def segment_terms(queries, keys, directions, beta):
    length, head_count, head_width = queries.shape
    raw_dirs = directions.astype(jnp.float32)
    unit_dirs = raw_dirs * lax.rsqrt(lax.optimization_barrier(jnp.sum(raw_dirs * raw_dirs, axis=1, keepdims=True)) + 1e-06)
    positions = jnp.arange(length)
    strict_mask = positions[:, None] > positions[None, :]
    causal_mask = positions[:, None] >= positions[None, :]
    intersections = jnp.where(strict_mask, jnp.dot(unit_dirs, unit_dirs.T, precision=exact_mode), 0.0)
    identity = jnp.eye(length, dtype=jnp.float32)
    scaled_dirs = beta[:, None] * unit_dirs
    keys_wide = keys.astype(jnp.float32)
    key_reach = jnp.where(strict_mask, jnp.dot(unit_dirs, keys_wide.T, precision=exact_mode), 0.0)
    solution = jax.scipy.linalg.solve_triangular(identity + intersections * beta[None, :], jnp.concatenate([key_reach, unit_dirs], axis=1), lower=True, unit_diagonal=True)
    moved_keys = keys_wide - jnp.dot(solution[:, :length].T, scaled_dirs, precision=exact_mode)
    transform = jnp.eye(head_width, dtype=jnp.float32) - jnp.dot(unit_dirs.T, beta[:, None] * solution[:, length:], precision=exact_mode)
    queries_wide = queries.astype(jnp.float32)
    query_reach = jnp.einsum('te,ihe->thi', unit_dirs, queries_wide, precision=exact_mode)
    query_reach = jnp.where(causal_mask.T[:, None, :], query_reach, 0.0)
    coefficients = jax.scipy.linalg.solve_triangular(identity + beta[:, None] * intersections, query_reach.reshape(length, head_count * length), lower=True, trans=1, unit_diagonal=True).reshape(length, head_count, length)
    moved_queries = queries_wide - jnp.einsum('thi,te->ihe', coefficients, scaled_dirs, precision=exact_mode)
    plain_scores = jnp.einsum('ihe,je->ihj', queries_wide, keys_wide, precision=exact_mode)
    correction = jnp.einsum('thi,tj->ihj', coefficients, beta[:, None] * key_reach, precision=exact_mode)
    local_scores = jnp.where(causal_mask[:, None, :], (plain_scores - correction) * head_width ** (-0.5), -1e+30)
    return (moved_queries, moved_keys, transform, local_scores)

def group_output(queries, keys, values, directions, beta, gain):
    grouped = queries.reshape(N_SEQ, TOK_DEV, GROUP_HEADS, HD)

    def local_terms(pieces):
        return segment_terms(pieces[0], pieces[1], pieces[2], pieces[3])
    moved_queries, moved_keys, transforms, local_scores = lax.map(local_terms, (grouped, keys.reshape(N_SEQ, TOK_DEV, HD), directions.reshape(N_SEQ, TOK_DEV, HD), beta.reshape(N_SEQ, TOK_DEV)))
    query_rows = moved_queries.reshape(N_SEQ, TOK_DEV * GROUP_HEADS, HD).astype(jnp.bfloat16)
    local_flat = local_scores.reshape(N_SEQ, TOK_DEV * GROUP_HEADS, TOK_DEV)
    key_travel = moved_keys.astype(jnp.bfloat16)
    hop_matrices = transforms.astype(jnp.bfloat16)
    value_blocks = values.reshape(N_SEQ, TOK_DEV, HD)
    positions = jnp.arange(TOKENS)

    def attend_segment(history, inputs):
        segment_index, query_block, local_block, own_keys, own_values, hop_matrix = inputs
        cross = jnp.dot(query_block.astype(jnp.float32), history.T.astype(jnp.float32), preferred_element_type=jnp.float32) * HD ** (-0.5)
        cross = jnp.where((positions < segment_index * TOK_DEV)[None, :], cross, -1e+30)
        scores = jnp.concatenate([cross, local_block], axis=1)
        peak = lax.optimization_barrier(jnp.max(scores, axis=1, keepdims=True))
        weights_exp = jnp.exp(scores - peak)
        denominator = lax.optimization_barrier(jnp.sum(weights_exp, axis=1, keepdims=True))
        mixed = jnp.dot(weights_exp.astype(jnp.bfloat16).astype(jnp.float32), jnp.concatenate([values, own_values], axis=0).astype(jnp.float32), preferred_element_type=jnp.float32) / denominator
        strength = lax.rsqrt(lax.optimization_barrier(jnp.mean(mixed * mixed, axis=1, keepdims=True)) + 1e-06)
        normed = (mixed * strength * gain[None, :]).astype(jnp.bfloat16)
        history = jnp.dot(history.astype(jnp.float32), hop_matrix.T.astype(jnp.float32), preferred_element_type=jnp.float32).astype(jnp.bfloat16)
        history = lax.dynamic_update_slice(history, own_keys, ((segment_index * TOK_DEV).astype(jnp.int32), jnp.int32(0)))
        return (history, normed)
    history = jnp.zeros((TOKENS, HD), jnp.bfloat16)
    indices = jnp.arange(N_SEQ, dtype=jnp.int32)
    final_history, outputs = lax.scan(attend_segment, history, (indices, query_rows, local_flat, key_travel, value_blocks, hop_matrices))
    return outputs.reshape(TOKENS, GROUP_HEADS * HD)

def reference(queries, keys, values, directions, beta, gain):
    query_groups = queries.reshape(TOKENS, GROUPS, GROUP_HEADS * HD).transpose(1, 0, 2)
    key_groups = keys.reshape(TOKENS, GROUPS, HD).transpose(1, 0, 2)
    value_groups = values.reshape(TOKENS, GROUPS, HD).transpose(1, 0, 2)
    direction_groups = directions.reshape(TOKENS, GROUPS, HD).transpose(1, 0, 2)
    beta_groups = beta.T

    def one_group(pieces):
        return group_output(pieces[0], pieces[1], pieces[2], pieces[3], pieces[4], gain)
    outputs = lax.map(one_group, (query_groups, key_groups, value_groups, direction_groups, beta_groups))
    return outputs.transpose(1, 0, 2).reshape(TOKENS, HEADS * HD)
```

```python
import functools

import jax
import jax.numpy as jnp
from jax import lax
from jax.experimental import pallas as pl
from jax.experimental.pallas import tpu as pltpu
from jax.sharding import PartitionSpec as P

WIDE = jnp.float32
NARROW = jnp.bfloat16
MASKED = -1e30


def halves(x):
    top = x.astype(NARROW)
    return top, (x - top.astype(WIDE)).astype(NARROW)


def dot(a, b):
    return jnp.dot(a, b, preferred_element_type=WIDE)


def dot3(a, b):
    a_top, a_low = a
    b_top, b_low = b
    return dot(
        jnp.concatenate([a_top, a_low, a_top], axis=1),
        jnp.concatenate([b_top, b_top, b_low], axis=0),
    )


def prepare(own_ref, other_ref, beta_ref, pack_ref, solved_ref, sides_ref, coef_ref, full_ref):
    half, length = own_ref.shape[0] // 3, own_ref.shape[1]
    width = 2 * half
    place = lax.axis_index("head")
    parity = place % 2
    for part in range(3):
        rows = pl.ds(part * half, half)
        full_ref[part, pl.ds(parity * half, half), :] = own_ref[rows, :]
        full_ref[part, pl.ds((1 - parity) * half, half), :] = other_ref[rows, :]
    keys_t, values_t, dirs_t = full_ref[0], full_ref[1], full_ref[2]
    dirs_wide = dirs_t.astype(WIDE)
    dirs = dirs_wide.T.astype(NARROW)
    power = jnp.sum(dirs_wide * dirs_wide, axis=0, keepdims=True) + 1e-06
    coef = beta_ref[pl.ds(place // 2, 1), :] / power

    row = lax.broadcasted_iota(jnp.int32, (length, length), 0)
    col = lax.broadcasted_iota(jnp.int32, (length, length), 1)
    sides = jnp.concatenate([dirs_t, keys_t], axis=1)
    meets = dot(dirs, sides)
    below = jnp.where(row > col, meets[:, :length] * coef, 0.0)
    reach = jnp.where(row > col, meets[:, length:], 0.0)

    inverse = jnp.where(row == col, 1.0, 0.0) - jnp.where((row ^ col) == 1, below, 0.0)
    block = 2
    while block < length:
        joint = jnp.where((row // block) ^ (col // block) == 1, below, 0.0)
        parts = halves(inverse)
        inverse = inverse - dot3(parts, halves(dot3(halves(joint), parts)))
        block *= 2

    top, low = halves(inverse)
    reach_top, reach_low = halves(reach)
    right = jnp.concatenate([reach_top, dirs], axis=1)
    solved = dot(jnp.concatenate([top, low], axis=1), jnp.concatenate([right, right], axis=0))
    solved_reach = solved[:, :length] + dot(top, reach_low)
    solved = jnp.concatenate([solved_reach, solved[:, length:]], axis=1)
    solved_parts = halves(solved)
    change = dot3(halves(dirs_wide * coef), solved_parts)
    pack_ref[:, :length] = (keys_t.astype(WIDE) - change[:, :length]).astype(NARROW)
    row_w = lax.broadcasted_iota(jnp.int32, (width, width), 0)
    col_w = lax.broadcasted_iota(jnp.int32, (width, width), 1)
    unit = jnp.where(row_w == col_w, 1.0, 0.0)
    pack_ref[:, length : length + width] = (unit - change[:, length:]).astype(NARROW)
    pack_ref[:, length + width :] = values_t.astype(WIDE).T.astype(NARROW)
    solved_ref[0] = solved_parts[0]
    solved_ref[1] = solved_parts[1]
    sides_ref[...] = sides
    coef_ref[...] = jnp.broadcast_to(coef, coef_ref.shape)


def own_segment(queries_ref, solved_ref, sides_ref, coef_ref, moved_ref, local_ref):
    length = queries_ref.shape[0]
    width = sides_ref.shape[0]
    heads = queries_ref.shape[1] // width
    coef = coef_ref[:1, :]
    sides = sides_ref[...]
    top, low = solved_ref[0], solved_ref[1]
    right = jnp.concatenate([top, top, low], axis=0)
    row = lax.broadcasted_iota(jnp.int32, (length, length), 0)
    col = lax.broadcasted_iota(jnp.int32, (length, length), 1)
    for head in range(heads):
        cols = pl.ds(head * width, width)
        query = queries_ref[:, cols]
        plain = dot(query, sides)
        met = jnp.where(row >= col, plain[:, :length] * coef, 0.0)
        met_top, met_low = halves(met)
        change = dot(jnp.concatenate([met_top, met_low, met_top], axis=1), right)
        moved_ref[:, cols] = (query.astype(WIDE) - change[:, length:]).astype(NARROW)
        scores = (plain[:, length:] - change[:, :length]) * width ** (-0.5)
        local_ref[:, pl.ds(head * length, length)] = jnp.where(row >= col, scores, MASKED)


def attend(moved_ref, local_ref, all_ref, gain_ref, out_ref, keys_ref, values_ref):
    length = moved_ref.shape[0]
    width = gain_ref.shape[1]
    heads = moved_ref.shape[1] // width
    segments = all_ref.shape[0] // length
    place = lax.axis_index("seq")
    travel = None
    for step in range(1, segments):
        rows = pl.ds(pl.multiple_of(jnp.maximum(place - step, 0) * length, length), length)
        block = all_ref[rows, pl.ds(0, length + width)]
        at = pl.ds((step - 1) * length, length)
        values_ref[at, :] = all_ref[rows, pl.ds(length + width, width)]
        if step == 1:
            keys_ref[:, at] = block[:, :length]
            travel = block[:, length:].astype(WIDE)
        else:
            both = dot(
                jnp.concatenate(halves(travel), axis=1), jnp.concatenate([block, block], axis=0)
            )
            keys_ref[:, at] = both[:, :length].astype(NARROW)
            travel = both[:, length:]
    last = pl.ds((segments - 1) * length, length)
    values_ref[last, :] = all_ref[
        pl.ds(pl.multiple_of(place * length, length), length), pl.ds(length + width, width)
    ]
    gain = gain_ref[...]
    scale = width ** (-0.5)
    for head in range(heads):
        cols = pl.ds(head * width, width)
        cross = dot(moved_ref[:, cols], keys_ref[...]) * scale
        column = lax.broadcasted_iota(jnp.int32, cross.shape, 1)
        cross = jnp.where(column < place * length, cross, MASKED)
        scores = jnp.concatenate([cross, local_ref[:, pl.ds(head * length, length)]], axis=1)
        peak = jnp.max(scores, axis=1, keepdims=True)
        weights = jnp.exp(scores - peak)
        total = jnp.sum(weights, axis=1, keepdims=True)
        mixed = dot(weights.astype(NARROW), values_ref[...]) / total
        strength = lax.rsqrt(jnp.mean(mixed * mixed, axis=1, keepdims=True) + 1e-06)
        out_ref[:, cols] = (mixed * strength * gain).astype(NARROW)


def call(kernel, outs, scratch=(), flops=1e8):
    return pl.pallas_call(
        kernel,
        out_shape=outs,
        scratch_shapes=list(scratch),
        cost_estimate=pl.CostEstimate(
            flops=int(flops), bytes_accessed=1 << 20, transcendentals=1 << 17
        ),
    )


def shards(queries, keys, values, directions, beta, gain):
    length, half = directions.shape
    width = 2 * half
    heads = queries.shape[1] // width
    segments = lax.axis_size("seq")
    own = jnp.concatenate([keys.T, values.T, directions.T], axis=0)
    places = range(lax.axis_size("head"))
    other = lax.ppermute(own, "head", [(place, place ^ 1) for place in places])
    shape = jax.ShapeDtypeStruct
    pack, solved, sides, coef = call(
        prepare,
        (
            shape((width, 2 * length + width), NARROW),
            shape((2, length, length + width), NARROW),
            shape((width, 2 * length), NARROW),
            shape((8, length), WIDE),
        ),
        [pltpu.VMEM((3, width, length), NARROW)],
    )(own, other, beta.T)
    everyone = lax.all_gather(pack, "seq", tiled=True)
    moved, local = call(
        own_segment,
        (shape((length, heads * width), NARROW), shape((length, heads * length), WIDE)),
    )(queries, solved, sides, coef)
    return call(
        attend,
        shape((length, heads * width), NARROW),
        [
            pltpu.VMEM((width, (segments - 1) * length), NARROW),
            pltpu.VMEM((segments * length, width), NARROW),
        ],
        flops=1e9,
    )(moved, local, everyone, gain.reshape(1, -1))


def solution(mesh):
    placed = (
        P("seq", "head"),
        P("seq", "head"),
        P("seq", "head"),
        P("seq", "head"),
        P("seq", None),
        P(),
    )
    return jax.shard_map(
        shards, mesh=mesh, in_specs=placed, out_specs=P("seq", "head"), check_vma=False
    )
```

```python
import math

import jax
import jax.numpy as jnp
from jax import lax
from jax.experimental import pallas as pl
from jax.experimental.pallas import tpu as pltpu
from jax.sharding import PartitionSpec as P


WIDE = jnp.float32
NARROW = jnp.bfloat16
MASKED = -1e30


def halves(x):
    top = x.astype(NARROW)
    return top, (x - top.astype(WIDE)).astype(NARROW)


def dot(a, b):
    return jnp.dot(a, b, preferred_element_type=WIDE)


def dot3(a, b):
    a_top, a_low = a
    b_top, b_low = b
    return dot(
        jnp.concatenate([a_top, a_low, a_top], axis=1),
        jnp.concatenate([b_top, b_top, b_low], axis=0),
    )


def prepare(own_ref, other_ref, beta_ref, pack_ref, solved_ref, sides_ref, coef_ref, full_ref):
    half, length = own_ref.shape[0] // 3, own_ref.shape[1]
    width = 2 * half
    place = lax.axis_index("head")
    parity = place % 2
    for part in range(3):
        rows = pl.ds(part * half, half)
        full_ref[part, pl.ds(parity * half, half), :] = own_ref[rows, :]
        full_ref[part, pl.ds((1 - parity) * half, half), :] = other_ref[rows, :]
    keys_t, values_t, dirs_t = full_ref[0], full_ref[1], full_ref[2]
    dirs_wide = dirs_t.astype(WIDE)
    dirs = dirs_wide.T.astype(NARROW)
    power = jnp.sum(dirs_wide * dirs_wide, axis=0, keepdims=True) + 1e-06
    coef = beta_ref[...] / power

    row = lax.broadcasted_iota(jnp.int32, (length, length), 0)
    col = lax.broadcasted_iota(jnp.int32, (length, length), 1)
    sides = jnp.concatenate([dirs_t, keys_t], axis=1)
    meets = dot(dirs, sides)
    below = jnp.where(row > col, meets[:, :length] * coef, 0.0)
    reach = jnp.where(row > col, meets[:, length:], 0.0)

    inverse = jnp.where(row == col, 1.0, 0.0) - jnp.where((row ^ col) == 1, below, 0.0)
    block = 2
    while block < length:
        joint = jnp.where((row // block) ^ (col // block) == 1, below, 0.0)
        parts = halves(inverse)
        inverse = inverse - dot3(parts, halves(dot3(halves(joint), parts)))
        block *= 2

    top, low = halves(inverse)
    reach_top, reach_low = halves(reach)
    right = jnp.concatenate([reach_top, dirs], axis=1)
    solved = dot(jnp.concatenate([top, low], axis=1), jnp.concatenate([right, right], axis=0))
    solved_reach = solved[:, :length] + dot(top, reach_low)
    solved = jnp.concatenate([solved_reach, solved[:, length:]], axis=1)
    solved_parts = halves(solved)
    change = dot3(halves(dirs_wide * coef), solved_parts)
    pack_ref[:, :length] = (keys_t.astype(WIDE) - change[:, :length]).astype(NARROW)
    row_w = lax.broadcasted_iota(jnp.int32, (width, width), 0)
    col_w = lax.broadcasted_iota(jnp.int32, (width, width), 1)
    unit = jnp.where(row_w == col_w, 1.0, 0.0)
    pack_ref[:, length : length + width] = (unit - change[:, length:]).astype(NARROW)
    pack_ref[:, length + width :] = values_t.astype(WIDE).T.astype(NARROW)
    solved_ref[0] = solved_parts[0]
    solved_ref[1] = solved_parts[1]
    sides_ref[...] = sides
    coef_ref[...] = jnp.broadcast_to(coef, coef_ref.shape)


def own_segment(
    queries_ref, solved_ref, sides_ref, coef_ref, pack_ref, moved_ref, peak_ref, sum_ref, mix_ref
):
    length = queries_ref.shape[0]
    width = sides_ref.shape[0]
    heads = queries_ref.shape[1] // width
    coef = coef_ref[:1, :]
    sides = sides_ref[...]
    top, low = solved_ref[0], solved_ref[1]
    right = jnp.concatenate([top, top, low], axis=0)
    values = counted(pack_ref[:, length + width :])
    row = lax.broadcasted_iota(jnp.int32, (length, length), 0)
    col = lax.broadcasted_iota(jnp.int32, (length, length), 1)
    for head in range(heads):
        cols = pl.ds(head * width, width)
        query = queries_ref[:, cols]
        plain = dot(query, sides)
        met = jnp.where(row >= col, plain[:, :length] * coef, 0.0)
        met_top, met_low = halves(met)
        change = dot(jnp.concatenate([met_top, met_low, met_top], axis=1), right)
        moved_ref[:, cols] = (query.astype(WIDE) - change[:, length:]).astype(NARROW)
        scores = jnp.where(row >= col, plain[:, length:] - change[:, :length], MASKED)
        peak = jnp.max(scores, axis=1, keepdims=True)
        mixed = dot(powers(scores, peak, width).astype(NARROW), values)
        peak_ref[:, cols] = jnp.broadcast_to(peak, (length, width))
        mix_ref[:, cols] = mixed[:, :width]
        sum_ref[:, cols] = mixed[:, width:]


def counted(values):
    return jnp.concatenate([values, jnp.ones_like(values)], axis=1)


def powers(scores, peak, width):
    return jnp.exp2((scores - peak) * (width ** (-0.5) * math.log2(math.e)))


def carry(travel, block, length):
    both = dot(jnp.concatenate(halves(travel), axis=1), jnp.concatenate([block, block], axis=0))
    return both[:, :length].astype(NARROW), both[:, length:]


def take_in(head, moved_ref, keys, values, peak, total, mix, width):
    scores = dot(moved_ref[:, pl.ds(head * width, width)], keys)
    above = jnp.maximum(peak, jnp.max(scores, axis=1, keepdims=True))
    fade = powers(peak, above, width)
    mixed = dot(powers(scores, above[:, :1], width).astype(NARROW), values)
    return above, total * fade + mixed[:, width:], mix * fade + mixed[:, :width]


def attend(*refs):
    moved_ref, peak_ref, sum_ref, mix_ref, gain_hbm, mate_ref = refs[:6]
    out_ref, keys_ref, values_ref, done_ref, gain_ref, sem, gain_sem = refs[-7:]
    far = refs[6:-7]
    width, length = keys_ref.shape[0], moved_ref.shape[0]
    heads = moved_ref.shape[1] // width
    chips = len(far) // 2
    place = lax.axis_index("seq")
    core = place % 2
    chip_place = place // 2
    fetch = pltpu.make_async_copy(gain_hbm, gain_ref, gain_sem)
    fetch.start()

    def grab(ref, slot):
        if isinstance(ref, tuple):
            block = jnp.where(core == 1, ref[0][...], ref[1][...])
        else:
            block = ref[...]
        at = pl.ds(slot * length, length)
        values_ref[at, :] = counted(block[:, length + width :])
        return block[:, : length + width], at

    def state(head):
        cols = pl.ds(head * width, width)
        return peak_ref[:, cols], sum_ref[:, cols], mix_ref[:, cols]

    def finish(head, total, mix):
        cols = pl.ds(head * width, width)
        mixed = mix / total
        strength = lax.rsqrt(jnp.mean(mixed * mixed, axis=1, keepdims=True) + 1e-06)
        done_ref[:, cols] = (mixed * strength * gain_ref[...]).astype(NARROW)
        pltpu.make_async_copy(
            done_ref.at[:, cols], out_ref.at[:, cols], sem.at[head]
        ).start()

    @pl.when(chip_place > 0)
    def _():
        row = lax.broadcasted_iota(jnp.int32, (width, width), 0)
        col = lax.broadcasted_iota(jnp.int32, (width, width), 1)
        order = [mate_ref]
        for chip in range(chips):
            straight, crossed = far[2 * chip], far[2 * chip + 1]
            order += [(straight, crossed), (crossed, straight)]
        travel = None
        for slot, ref in enumerate(order):
            block, at = grab(ref, slot)
            if slot == 0:
                keys_ref[:, at] = block[:, :length]
                near = block[:, length:].astype(WIDE)
                travel = jnp.where(core == 1, near, jnp.where(row == col, 1.0, 0.0))
            else:
                keys_ref[:, at], travel = carry(travel, block, length)
        first, last = (1 - core) * length, (1 + 2 * chip_place) * length
        fetch.wait()
        for head in range(heads):
            peak, total, mix = state(head)
            scores = dot(moved_ref[:, pl.ds(head * width, width)], keys_ref[...])
            column = lax.broadcasted_iota(jnp.int32, scores.shape, 1)
            scores = jnp.where((column >= first) & (column < last), scores, MASKED)
            above = jnp.maximum(peak, jnp.max(scores, axis=1, keepdims=True))
            fade = powers(peak, above, width)
            mixed = dot(powers(scores, above[:, :1], width).astype(NARROW), values_ref[...])
            finish(head, total * fade + mixed[:, width:], mix * fade + mixed[:, :width])

    @pl.when((chip_place == 0) & (core == 1))
    def _():
        block, at = grab(mate_ref, 0)
        fetch.wait()
        for head in range(heads):
            _, total, mix = take_in(
                head, moved_ref, block[:, :length], values_ref[at, :], *state(head), width
            )
            finish(head, total, mix)

    @pl.when((chip_place == 0) & (core == 0))
    def _():
        fetch.wait()
        for head in range(heads):
            _, total, mix = state(head)
            finish(head, total, mix)

    for head in range(heads):
        cols = pl.ds(head * width, width)
        pltpu.make_async_copy(done_ref.at[:, cols], out_ref.at[:, cols], sem.at[head]).wait()


LOCAL = pl.BlockSpec(memory_space=pltpu.VMEM)
ANYWHERE = pl.BlockSpec(memory_space=pltpu.HBM)


def call(kernel, outs, count, scratch=(), flops=1e8, spots=None, far=()):
    return pl.pallas_call(
        kernel,
        out_shape=outs,
        in_specs=[ANYWHERE if i in far else LOCAL for i in range(count)],
        out_specs=spots or jax.tree.map(lambda _: LOCAL, outs),
        scratch_shapes=list(scratch),
        compiler_params=pltpu.CompilerParams(vmem_limit_bytes=16 << 20),
        cost_estimate=pl.CostEstimate(
            flops=int(flops), bytes_accessed=1 << 20, transcendentals=1 << 17
        ),
    )


def shards(queries, keys, values, directions, beta, gain):
    length, half = directions.shape
    width = 2 * half
    heads = queries.shape[1] // width
    segments = lax.axis_size("seq")
    own = jnp.concatenate([keys.T, values.T, directions.T], axis=0)
    places = range(lax.axis_size("head"))
    other = lax.ppermute(own, "head", [(place, place ^ 1) for place in places])
    shape = jax.ShapeDtypeStruct
    group = lax.axis_index("head") // 2
    chosen = jnp.arange(beta.shape[1]) == group
    strengths = jnp.sum(jnp.where(chosen[:, None], beta.T, 0.0), axis=0, keepdims=True)
    pack, solved, sides, coef = call(
        prepare,
        (
            shape((width, 2 * length + width), NARROW),
            shape((2, length, length + width), NARROW),
            shape((width, 2 * length), NARROW),
            shape((8, length), WIDE),
        ),
        3,
        [pltpu.VMEM((3, width, length), NARROW)],
    )(own, other, strengths)

    def across(block):
        return lax.ppermute(block, "seq", [(i, i ^ 1) for i in range(segments)])

    mate = across(pack)
    far = []
    for chip in range(1, segments // 2):
        pairs = [(i, (i + 2 * chip) % segments) for i in range(segments)]
        far.append(lax.ppermute(pack, "seq", pairs))
    moved, *state = call(
        own_segment,
        (shape((length, heads * width), NARROW),)
        + (shape((length, heads * width), WIDE),) * 3,
        5,
    )(queries, solved, sides, coef, pack)
    blocks = []
    for block in far:
        blocks += [block, across(block)]
    return call(
        attend,
        shape((length, heads * width), NARROW),
        6 + len(blocks),
        [
            pltpu.VMEM((width, (segments - 1) * length), NARROW),
            pltpu.VMEM(((segments - 1) * length, 2 * width), NARROW),
            pltpu.VMEM((length, heads * width), NARROW),
            pltpu.VMEM((1, width), WIDE),
            pltpu.SemaphoreType.DMA((heads,)),
            pltpu.SemaphoreType.DMA,
        ],
        flops=1e9,
        spots=ANYWHERE,
        far=(4,),
    )(moved, *state, gain.reshape(1, -1), mate, *blocks)


def solution(mesh):
    placed = (
        P("seq", "head"),
        P("seq", "head"),
        P("seq", "head"),
        P("seq", "head"),
        P("seq", None),
        P(),
    )

    return jax.shard_map(
        shards, mesh=mesh, in_specs=placed, out_specs=P("seq", "head"), check_vma=False
    )
```

```python
import math

import jax
import jax.numpy as jnp
from jax import lax
from jax.experimental import pallas as pl
from jax.experimental.pallas import tpu as pltpu
from jax.sharding import PartitionSpec as P


WIDE = jnp.float32
NARROW = jnp.bfloat16
MASKED = -1e30
OWN_PIECES, NEAR_PIECES, FAR_PIECES = 1,2,4


def halves(x):
    top = x.astype(NARROW)
    return top, (x - top.astype(WIDE)).astype(NARROW)


def dot(a, b):
    return jnp.dot(a, b, preferred_element_type=WIDE)


def dot3(a, b):
    a_top, a_low = a
    b_top, b_low = b
    return dot(
        jnp.concatenate([a_top, a_low, a_top], axis=1),
        jnp.concatenate([b_top, b_top, b_low], axis=0),
    )


def prepare(own_ref, other_ref, small_ref, pack_ref, solved_ref, sides_ref, coef_ref, full_ref):
    half, length = own_ref.shape[0] // 3, own_ref.shape[1]
    width = 2 * half
    place = lax.axis_index("head")
    parity = place % 2
    for part in range(3):
        rows = pl.ds(part * half, half)
        full_ref[part, pl.ds(parity * half, half), :] = own_ref[rows, :]
        full_ref[part, pl.ds((1 - parity) * half, half), :] = other_ref[rows, :]
    keys_t, values_t, dirs_t = full_ref[0], full_ref[1], full_ref[2]
    dirs_wide = dirs_t.astype(WIDE)
    dirs = dirs_wide.T.astype(NARROW)
    power = jnp.sum(dirs_wide * dirs_wide, axis=0, keepdims=True) + 1e-06
    coef = small_ref[:1, :] / power

    row = lax.broadcasted_iota(jnp.int32, (length, length), 0)
    col = lax.broadcasted_iota(jnp.int32, (length, length), 1)
    sides = jnp.concatenate([dirs_t, keys_t], axis=1)
    meets = dot(dirs, sides)
    below = jnp.where(row > col, meets[:, :length] * coef, 0.0)
    reach = jnp.where(row > col, meets[:, length:], 0.0)

    inverse = jnp.where(row == col, 1.0, 0.0) - jnp.where((row ^ col) == 1, below, 0.0)
    block = 2
    while block < length:
        joint = jnp.where((row // block) ^ (col // block) == 1, below, 0.0)
        parts = halves(inverse)
        inverse = inverse - dot3(parts, halves(dot3(halves(joint), parts)))
        block *= 2

    top, low = halves(inverse)
    reach_top, reach_low = halves(reach)
    right = jnp.concatenate([reach_top, dirs], axis=1)
    solved = dot(jnp.concatenate([top, low], axis=1), jnp.concatenate([right, right], axis=0))
    solved_reach = solved[:, :length] + dot(top, reach_low)
    solved = jnp.concatenate([solved_reach, solved[:, length:]], axis=1)
    solved_parts = halves(solved)
    change = dot3(halves(dirs_wide * coef), solved_parts)
    pack_ref[:, :length] = (keys_t.astype(WIDE) - change[:, :length]).astype(NARROW)
    row_w = lax.broadcasted_iota(jnp.int32, (width, width), 0)
    col_w = lax.broadcasted_iota(jnp.int32, (width, width), 1)
    unit = jnp.where(row_w == col_w, 1.0, 0.0)
    pack_ref[:, length : length + width] = (unit - change[:, length:]).astype(NARROW)
    pack_ref[:, length + width :] = values_t.astype(WIDE).T.astype(NARROW)
    solved_ref[0] = solved_parts[0]
    solved_ref[1] = solved_parts[1]
    sides_ref[...] = sides
    coef_ref[...] = jnp.broadcast_to(coef, coef_ref.shape)


def own_segment(
    queries_ref, solved_ref, sides_ref, coef_ref, pack_ref, moved_ref, peak_ref, sum_ref, mix_ref
):
    length = queries_ref.shape[0]
    width = sides_ref.shape[0]
    top, low = solved_ref[0], solved_ref[1]
    right = jnp.concatenate([top, top, low], axis=0)
    values = counted(pack_ref[:, length + width :])
    for part in pieces(moved_ref.shape[0], OWN_PIECES):
        heads = range(part.start // length, (part.start + part.size) // length)
        query = jnp.concatenate([queries_ref[:, pl.ds(h * width, width)] for h in heads], axis=0)
        row = lax.broadcasted_iota(jnp.int32, (part.size, length), 0) % length
        col = lax.broadcasted_iota(jnp.int32, (part.size, length), 1)
        past = row >= col
        plain = dot(query, sides_ref[...])
        met_top, met_low = halves(jnp.where(past, plain[:, :length] * coef_ref[:1, :], 0.0))
        change = dot(jnp.concatenate([met_top, met_low, met_top], axis=1), right)
        moved_ref[part, :] = (query.astype(WIDE) - change[:, length:]).astype(NARROW)
        scores = jnp.where(past, plain[:, length:] - change[:, :length], MASKED)
        peak = jnp.max(scores, axis=1, keepdims=True)
        mixed = dot(powers(scores, peak, width).astype(NARROW), values)
        peak_ref[part, :] = jnp.broadcast_to(peak, (part.size, width))
        mix_ref[part, :] = mixed[:, :width]
        sum_ref[part, :] = mixed[:, width:]


def counted(values):
    return jnp.concatenate([values, jnp.ones_like(values)], axis=1)


def powers(scores, peak, width):
    return jnp.exp2((scores - peak) * (width ** (-0.5) * math.log2(math.e)))


def carry(travel, block, length):
    both = dot(jnp.concatenate(halves(travel), axis=1), jnp.concatenate([block, block], axis=0))
    return both[:, :length].astype(NARROW), both[:, length:]


def gather(refs, core, keys_ref, values_ref, travel, length):
    width = keys_ref.shape[0]
    for slot, ref in enumerate(refs):
        if isinstance(ref, tuple):
            block = jnp.where(core == 1, ref[0][...], ref[1][...])
        else:
            block = ref[...]
        at = pl.ds(slot * length, length)
        values_ref[at, :] = counted(block[:, length + width :])
        block = block[:, : length + width]
        if travel is None:
            keys_ref[:, at] = block[:, :length]
            row = lax.broadcasted_iota(jnp.int32, (width, width), 0)
            col = lax.broadcasted_iota(jnp.int32, (width, width), 1)
            unit = jnp.where(row == col, 1.0, 0.0)
            travel = jnp.where(core == 1, block[:, length:].astype(WIDE), unit)
        else:
            keys_ref[:, at], travel = carry(travel, block, length)
    return travel


def take_in(query, keys, values, first, last, peak, total, mix):
    width = mix.shape[1]
    scores = dot(query, keys)
    column = lax.broadcasted_iota(jnp.int32, scores.shape, 1)
    scores = jnp.where((column >= first) & (column < last), scores, MASKED)
    above = jnp.maximum(peak, jnp.max(scores, axis=1, keepdims=True))
    fade = powers(peak, above, width)
    level = jnp.concatenate([above] * (scores.shape[1] // width), axis=1)
    mixed = dot(powers(scores, level, width).astype(NARROW), values)
    return above, total * fade + mixed[:, width:], mix * fade + mixed[:, :width]


def pieces(rows, count):
    size = rows // count
    return [pl.ds(start, size) for start in range(0, rows, size)]


def attend_near(
    moved_ref, peak_ref, sum_ref, mix_ref, mate_ref, straight_ref, crossed_ref,
    peak_out, sum_out, mix_out, travel_out, keys_ref, values_ref,
):
    width = keys_ref.shape[0]
    length = mate_ref.shape[1] - 2 * width
    place = lax.axis_index("seq")
    core, chip_place = place % 2, place // 2
    order = [mate_ref, (straight_ref, crossed_ref), (crossed_ref, straight_ref)]
    travel_out[...] = gather(order, core, keys_ref, values_ref, None, length)
    first = (1 - core) * length
    last = jnp.where(chip_place > 0, 3, 1) * length
    for part in pieces(moved_ref.shape[0], NEAR_PIECES):
        peak_out[part, :], sum_out[part, :], mix_out[part, :] = take_in(
            moved_ref[part, :], keys_ref[...], values_ref[...], first, last,
            peak_ref[part, :], sum_ref[part, :], mix_ref[part, :],
        )


def attend_far(*refs):
    moved_ref, peak_ref, sum_ref, mix_ref, travel_ref, small_ref = refs[:6]
    out_ref, keys_ref, values_ref, done_ref, sem = refs[-5:]
    far = refs[6:-5]
    length, width = out_ref.shape[0], keys_ref.shape[0]
    heads = out_ref.shape[1] // width
    place = lax.axis_index("seq")
    core, chip_place = place % 2, place // 2

    def out_copy(head):
        cols = pl.ds(head * width, width)
        return pltpu.make_async_copy(done_ref.at[:, cols], out_ref.at[:, cols], sem.at[head])

    def finish(part, total, mix):
        square = jnp.mean(mix * mix, axis=1, keepdims=True)
        strength = lax.rsqrt(square + 1e-06 * (total * total))
        normed = (mix * strength * small_ref[1:2, :]).astype(NARROW)
        for at in range(0, part.size, length):
            head = (part.start + at) // length
            done_ref[:, pl.ds(head * width, width)] = normed[at : at + length]
            out_copy(head).start()

    @pl.when(chip_place > 1)
    def _():
        order = []
        for straight, crossed in zip(far[::2], far[1::2]):
            order += [(straight, crossed), (crossed, straight)]
        gather(order, core, keys_ref, values_ref, travel_ref[...], length)
        last = 2 * (chip_place - 1) * length
        for part in pieces(moved_ref.shape[0], FAR_PIECES):
            _, total, mix = take_in(
                moved_ref[part, :], keys_ref[...], values_ref[...], 0, last,
                peak_ref[part, :], sum_ref[part, :], mix_ref[part, :],
            )
            finish(part, total, mix)

    @pl.when(chip_place <= 1)
    def _():
        for part in pieces(moved_ref.shape[0], heads):
            finish(part, sum_ref[part, :], mix_ref[part, :])

    for head in range(heads):
        out_copy(head).wait()


LOCAL = pl.BlockSpec(memory_space=pltpu.VMEM)
ANYWHERE = pl.BlockSpec(memory_space=pltpu.HBM)


def call(kernel, outs, count, scratch=(), flops=1e8, spots=None):
    return pl.pallas_call(
        kernel,
        out_shape=outs,
        in_specs=[LOCAL] * count,
        out_specs=spots or jax.tree.map(lambda _: LOCAL, outs),
        scratch_shapes=list(scratch),
        compiler_params=pltpu.CompilerParams(vmem_limit_bytes=16 << 20),
        cost_estimate=pl.CostEstimate(
            flops=int(flops), bytes_accessed=1 << 20, transcendentals=1 << 17
        ),
    )


def shards(queries, keys, values, directions, beta, gain):
    length, half = directions.shape
    width = 2 * half
    heads = queries.shape[1] // width
    segments = lax.axis_size("seq")
    own = jnp.concatenate([keys.T, values.T, directions.T], axis=0)
    places = range(lax.axis_size("head"))
    other = lax.ppermute(own, "head", [(place, place ^ 1) for place in places])
    shape = jax.ShapeDtypeStruct
    group = lax.axis_index("head") // 2
    chosen = jnp.arange(beta.shape[1]) == group
    strengths = jnp.sum(jnp.where(chosen[:, None], beta.T, 0.0), axis=0, keepdims=True)
    small = jnp.concatenate([strengths, gain.reshape(1, -1)], axis=0)
    pack, solved, sides, coef = call(
        prepare,
        (
            shape((width, 2 * length + width), NARROW),
            shape((2, length, length + width), NARROW),
            shape((width, 2 * length), NARROW),
            shape((8, length), WIDE),
        ),
        3,
        [pltpu.VMEM((3, width, length), NARROW)],
    )(own, other, small)

    def across(block):
        return lax.ppermute(block, "seq", [(i, i ^ 1) for i in range(segments)])

    mate = across(pack)
    chips = segments // 2
    far = []
    for chip in range(1, chips):
        pairs = [(i, (i + 2 * chip) % segments) for i in range(segments)]
        far.append(lax.ppermute(pack, "seq", pairs))
    state_shape = (shape((heads * length, width), WIDE),) * 3
    moved, *state = call(
        own_segment, (shape((heads * length, width), NARROW),) + state_shape, 5
    )(queries, solved, sides, coef, pack)

    def stores(count):
        return [
            pltpu.VMEM((width, count * length), NARROW),
            pltpu.VMEM((count * length, 2 * width), NARROW),
        ]

    crossed = across(far[0])
    *state, travel = call(
        attend_near, state_shape + (shape((width, width), WIDE),), 7, stores(3)
    )(moved, *state, mate, far[0], crossed)
    blocks = []
    for chip in range(2, chips):
        blocks += [far[chip - 1], across(far[chip - 1])]
    return call(
        attend_far,
        shape((length, heads * width), NARROW),
        6 + len(blocks),
        stores(2 * (chips - 2))
        + [pltpu.VMEM((length, heads * width), NARROW), pltpu.SemaphoreType.DMA((heads,))],
        flops=1e9,
        spots=ANYWHERE,
    )(moved, *state, travel, small, *blocks)


def solution(mesh):
    placed = (
        P("seq", "head"),
        P("seq", "head"),
        P("seq", "head"),
        P("seq", "head"),
        P("seq", None),
        P(),
    )

    return jax.shard_map(
        shards, mesh=mesh, in_specs=placed, out_specs=P("seq", "head"), check_vma=False
    )
```

```python
import math

import jax
import jax.numpy as jnp
from jax import lax
from jax.experimental import pallas as pl
from jax.experimental.pallas import tpu as pltpu
from jax.sharding import PartitionSpec as P


WIDE = jnp.float32
NARROW = jnp.bfloat16
MASKED = -1e30
LAST_PIECES, LAST_GROUPS = 4, 2
OWN_PIECES, NEAR_PIECES = 1, 2


def halves(x):
    top = x.astype(NARROW)
    return top, (x - top.astype(WIDE)).astype(NARROW)


def dot(a, b):
    return jnp.dot(a, b, preferred_element_type=WIDE)


def dot3(a, b):
    a_top, a_low = a
    b_top, b_low = b
    return dot(
        jnp.concatenate([a_top, a_low, a_top], axis=1),
        jnp.concatenate([b_top, b_top, b_low], axis=0),
    )


def whole(full_ref, own, other, parity):
    half = own.shape[0]
    full_ref[pl.ds(parity * half, half), :] = own
    full_ref[pl.ds((1 - parity) * half, half), :] = other
    return full_ref[...]


def invert(own_ref, other_ref, small_ref, inverse_ref, across_ref, dirs_ref, coef_ref, full_ref):
    length = own_ref.shape[1]
    place = lax.axis_index("head")
    parity = place % 2
    dirs_t = whole(full_ref, own_ref[...], other_ref[...], parity)
    across_ref[...] = dirs_t
    dirs_wide = dirs_t.astype(WIDE)
    dirs = dirs_wide.T.astype(NARROW)
    dirs_ref[...] = dirs
    power = jnp.sum(dirs_wide * dirs_wide, axis=0, keepdims=True) + 1e-06
    coef = small_ref[pl.ds(place // 2, 1), :] / power
    coef_ref[...] = jnp.broadcast_to(coef, coef_ref.shape)

    row = lax.broadcasted_iota(jnp.int32, (length, length), 0)
    col = lax.broadcasted_iota(jnp.int32, (length, length), 1)
    below = jnp.where(row > col, dot(dirs, dirs_t) * coef, 0.0)

    inverse = jnp.where(row == col, 1.0, 0.0) - jnp.where((row ^ col) == 1, below, 0.0)
    block = 2
    while block < length:
        joint = halves(jnp.where((row // block) ^ (col // block) == 1, below, 0.0))
        parts = halves(inverse)
        step = block if block % 8 == 0 else length
        starts = range(step % length, length, 2 * step)
        lower = [jnp.concatenate([p[s : s + step] for s in starts], axis=0) for p in parts]
        change = dot3(halves(dot3(lower, joint)), parts)
        if step == length:
            inverse = inverse - change
        else:
            rows = []
            for at, start in enumerate(starts):
                rows.append(inverse[start - step : start])
                rows.append(inverse[start : start + step] - change[at * step : (at + 1) * step])
            inverse = jnp.concatenate(rows, axis=0)
        block *= 2
    inverse_ref[0], inverse_ref[1] = halves(inverse)


def prepare(
    own_ref, other_ref, inverse_ref, across_ref, dirs_ref, coef_ref,
    pack_ref, solved_ref, sides_ref, full_ref,
):
    half, length = own_ref.shape[0] // 2, own_ref.shape[1]
    width = 2 * half
    parity = lax.axis_index("head") % 2
    keys_t = whole(full_ref.at[0], own_ref[:half, :], other_ref[:half, :], parity)
    values_t = whole(full_ref.at[1], own_ref[half:, :], other_ref[half:, :], parity)
    dirs_t, dirs = across_ref[...], dirs_ref[...]
    row = lax.broadcasted_iota(jnp.int32, (length, length), 0)
    col = lax.broadcasted_iota(jnp.int32, (length, length), 1)
    top, low = inverse_ref[0], inverse_ref[1]
    reach_top, reach_low = halves(jnp.where(row > col, dot(dirs, keys_t), 0.0))
    right = jnp.concatenate([reach_top, dirs], axis=1)
    solved = dot(jnp.concatenate([top, low], axis=1), jnp.concatenate([right, right], axis=0))
    solved_reach = solved[:, :length] + dot(top, reach_low)
    solved_parts = halves(jnp.concatenate([solved_reach, solved[:, length:]], axis=1))
    change = dot3(halves(dirs_t.astype(WIDE) * coef_ref[:1, :]), solved_parts)
    pack_ref[:, :length] = (keys_t.astype(WIDE) - change[:, :length]).astype(NARROW)
    row_w = lax.broadcasted_iota(jnp.int32, (width, width), 0)
    col_w = lax.broadcasted_iota(jnp.int32, (width, width), 1)
    unit = jnp.where(row_w == col_w, 1.0, 0.0)
    pack_ref[:, length : length + width] = (unit - change[:, length:]).astype(NARROW)
    pack_ref[:, length + width :] = values_t.astype(WIDE).T.astype(NARROW)
    solved_ref[0] = solved_parts[0]
    solved_ref[1] = solved_parts[1]
    sides_ref[...] = jnp.concatenate([dirs_t, keys_t], axis=1)


def own_segment(
    queries_ref, solved_ref, sides_ref, coef_ref, pack_ref, moved_ref, peak_ref, sum_ref, mix_ref
):
    length = queries_ref.shape[0]
    width = sides_ref.shape[0]
    top, low = solved_ref[0], solved_ref[1]
    right = jnp.concatenate([top, top, low], axis=0)
    values = counted(pack_ref[:, length + width :])
    for part in pieces(moved_ref.shape[0], OWN_PIECES):
        heads = range(part.start // length, (part.start + part.size) // length)
        query = jnp.concatenate([queries_ref[:, pl.ds(h * width, width)] for h in heads], axis=0)
        row = lax.broadcasted_iota(jnp.int32, (part.size, length), 0) % length
        col = lax.broadcasted_iota(jnp.int32, (part.size, length), 1)
        past = row >= col
        plain = dot(query, sides_ref[...])
        met_top, met_low = halves(jnp.where(past, plain[:, :length] * coef_ref[:1, :], 0.0))
        change = dot(jnp.concatenate([met_top, met_low, met_top], axis=1), right)
        moved_ref[part, :] = (query.astype(WIDE) - change[:, length:]).astype(NARROW)
        scores = jnp.where(past, plain[:, length:] - change[:, :length], MASKED)
        peak = jnp.max(scores, axis=1, keepdims=True)
        mixed = dot(powers(scores, peak, width).astype(NARROW), values)
        peak_ref[part, :] = jnp.broadcast_to(peak, (part.size, width))
        mix_ref[part, :] = mixed[:, :width]
        sum_ref[part, :] = mixed[:, width:]


def counted(values):
    return jnp.concatenate([values, jnp.ones_like(values)], axis=1)


def powers(scores, peak, width):
    return jnp.exp2((scores - peak) * (width ** (-0.5) * math.log2(math.e)))


def carry(travel, block, length):
    both = dot(jnp.concatenate(halves(travel), axis=1), jnp.concatenate([block, block], axis=0))
    return both[:, :length].astype(NARROW), both[:, length:]


def gather(refs, core, keys_ref, values_ref, travel, length):
    width = keys_ref.shape[0]
    for slot, ref in enumerate(refs):
        if isinstance(ref, tuple):
            block = jnp.where(core == 1, ref[0][...], ref[1][...])
        else:
            block = ref[...]
        at = pl.ds(slot * length, length)
        values_ref[at, :] = counted(block[:, length + width :])
        block = block[:, : length + width]
        if travel is None:
            keys_ref[:, at] = block[:, :length]
            row = lax.broadcasted_iota(jnp.int32, (width, width), 0)
            col = lax.broadcasted_iota(jnp.int32, (width, width), 1)
            unit = jnp.where(row == col, 1.0, 0.0)
            travel = jnp.where(core == 1, block[:, length:].astype(WIDE), unit)
        else:
            keys_ref[:, at], travel = carry(travel, block, length)
    return travel


def pairs_of(far):
    order = []
    for straight, crossed in zip(far[::2], far[1::2]):
        order += [(straight, crossed), (crossed, straight)]
    return order


def take_in(query, keys, values, limits, peak, total, mix):
    width = mix.shape[1]
    scores = dot(query, keys)
    if limits is not None:
        column = lax.broadcasted_iota(jnp.int32, scores.shape, 1)
        scores = jnp.where((column >= limits[0]) & (column < limits[1]), scores, MASKED)
    above = jnp.maximum(peak, jnp.max(scores, axis=1, keepdims=True))
    fade = powers(peak, above, width)
    level = jnp.concatenate([above] * (scores.shape[1] // width), axis=1)
    mixed = dot(powers(scores, level, width).astype(NARROW), values)
    return above, total * fade + mixed[:, width:], mix * fade + mixed[:, :width]


def pieces(rows, count):
    size = rows // count
    return [pl.ds(start, size) for start in range(0, rows, size)]


def attend_near(
    moved_ref, peak_ref, sum_ref, mix_ref, mate_ref, straight_ref, crossed_ref,
    peak_out, sum_out, mix_out, travel_out, keys_ref, values_ref,
):
    width = keys_ref.shape[0]
    length = mate_ref.shape[1] - 2 * width
    place = lax.axis_index("seq")
    core, chip_place = place % 2, place // 2

    def absorb(span, limits):
        for part in pieces(moved_ref.shape[0], NEAR_PIECES):
            peak_out[part, :], sum_out[part, :], mix_out[part, :] = take_in(
                moved_ref[part, :], keys_ref[:, span], values_ref[span, :], limits,
                peak_ref[part, :], sum_ref[part, :], mix_ref[part, :],
            )

    @pl.when(chip_place > 0)
    def _():
        order = [mate_ref] + pairs_of([straight_ref, crossed_ref])
        travel_out[...] = gather(order, core, keys_ref, values_ref, None, length)
        absorb(pl.ds(0, 3 * length), ((1 - core) * length, 3 * length))

    @pl.when((chip_place == 0) & (core == 1))
    def _():
        gather([mate_ref], core, keys_ref, values_ref, None, length)
        absorb(pl.ds(0, length), None)


def attend_last(*refs):
    moved_ref, peak_ref, sum_ref, mix_ref, travel_ref, small_ref = refs[:6]
    out_ref, keys_ref, values_ref, done_ref, sem = refs[-5:]
    far = refs[6:-5]
    length, width = out_ref.shape[0], keys_ref.shape[0]
    heads = out_ref.shape[1] // width
    place = lax.axis_index("seq")
    core, chip_place = place % 2, place // 2

    def out_copy(head):
        cols = pl.ds(head * width, width)
        return pltpu.make_async_copy(done_ref.at[:, cols], out_ref.at[:, cols], sem.at[head])

    def finish(part, total, mix):
        square = jnp.mean(mix * mix, axis=1, keepdims=True)
        strength = lax.rsqrt(square + 1e-06 * (total * total))
        normed = (mix * strength * small_ref[small_ref.shape[0] - 1 :, :]).astype(NARROW)
        for at in range(0, part.size, length):
            head = (part.start + at) // length
            done_ref[:, pl.ds(head * width, width)] = normed[at : at + length]

    def run(states):
        parts = pieces(moved_ref.shape[0], LAST_PIECES)
        group = len(parts) // LAST_GROUPS
        for at in range(0, len(parts), group):
            for part in parts[at : at + group]:
                finish(part, *states(part))
            first = parts[at].start // length
            for head in range(first, first + group * parts[at].size // length):
                out_copy(head).start()

    @pl.when(chip_place > 1)
    def _():
        gather(pairs_of(far), core, keys_ref, values_ref, travel_ref[...], length)
        limits = (0, 2 * (chip_place - 1) * length) if len(far) > 2 else None
        run(
            lambda part: take_in(
                moved_ref[part, :], keys_ref[...], values_ref[...], limits,
                peak_ref[part, :], sum_ref[part, :], mix_ref[part, :],
            )[1:]
        )

    @pl.when(jnp.logical_not(chip_place > 1))
    def _():
        run(lambda part: (sum_ref[part, :], mix_ref[part, :]))

    for head in range(heads):
        out_copy(head).wait()


LOCAL = pl.BlockSpec(memory_space=pltpu.VMEM)
ANYWHERE = pl.BlockSpec(memory_space=pltpu.HBM)


def call(kernel, outs, count, scratch=(), flops=1e8, spots=None, aliases=None):
    return pl.pallas_call(
        kernel,
        out_shape=outs,
        in_specs=[LOCAL] * count,
        out_specs=spots or jax.tree.map(lambda _: LOCAL, outs),
        scratch_shapes=list(scratch),
        input_output_aliases=aliases or {},
        compiler_params=pltpu.CompilerParams(vmem_limit_bytes=16 << 20),
        cost_estimate=pl.CostEstimate(
            flops=int(flops), bytes_accessed=1 << 20, transcendentals=1 << 17
        ),
    )


def shards(queries, keys, values, directions, beta, gain):
    length, half = directions.shape
    width = 2 * half
    heads = queries.shape[1] // width
    segments = lax.axis_size("seq")
    places = range(lax.axis_size("head"))

    def partner(block):
        return lax.ppermute(block, "head", [(place, place ^ 1) for place in places])

    other_dirs = partner(directions.T)
    own = jnp.concatenate([keys.T, values.T], axis=0)
    other = partner(own)
    shape = jax.ShapeDtypeStruct
    small = jnp.concatenate([beta.T, gain.reshape(1, -1)], axis=0)
    square = shape((width, length), NARROW)
    inverse, dirs_t, dirs, coef = call(
        invert,
        (shape((2, length, length), NARROW), square, square, shape((8, length), WIDE)),
        3,
        [pltpu.VMEM((width, length), NARROW)],
    )(directions.T, other_dirs, small)
    pack, solved, sides = call(
        prepare,
        (
            shape((width, 2 * length + width), NARROW),
            shape((2, length, length + width), NARROW),
            shape((width, 2 * length), NARROW),
        ),
        6,
        [pltpu.VMEM((2, width, length), NARROW)],
    )(own, other, inverse, dirs_t, dirs, coef)

    def across(block, first=0):
        return lax.ppermute(block, "seq", [(i, i ^ 1) for i in range(2 * first, segments)])

    mate = across(pack)
    chips = segments // 2
    far = []
    for chip in range(1, chips):
        pairs = [(i, (i + 2 * chip) % segments) for i in range(segments)]
        far.append(lax.ppermute(pack, "seq", pairs))
    state_shape = (shape((heads * length, width), WIDE),) * 3
    moved, *state = call(
        own_segment, (shape((heads * length, width), NARROW),) + state_shape, 5
    )(queries, solved, sides, coef, pack)

    def stores(count):
        return [
            pltpu.VMEM((width, count * length), NARROW),
            pltpu.VMEM((count * length, 2 * width), NARROW),
        ]

    crossed = across(far[0])
    states = state_shape + (shape((width, width), WIDE),)
    in_place = {1: 0, 2: 1, 3: 2}
    *state, travel = call(attend_near, states, 7, stores(3), aliases=in_place)(
        moved, *state, mate, far[0], crossed
    )
    blocks = []
    for chip in range(2, chips):
        blocks += [far[chip - 1], across(far[chip - 1])]
    return call(
        attend_last,
        shape((length, heads * width), NARROW),
        6 + len(blocks),
        stores(2 * (chips - 2))
        + [pltpu.VMEM((length, heads * width), NARROW), pltpu.SemaphoreType.DMA((heads,))],
        flops=1e9,
        spots=ANYWHERE,
    )(moved, *state, travel, small, *blocks)


def solution(mesh):
    placed = (
        P("seq", "head"),
        P("seq", "head"),
        P("seq", "head"),
        P("seq", "head"),
        P("seq", None),
        P(),
    )

    return jax.shard_map(
        shards, mesh=mesh, in_specs=placed, out_specs=P("seq", "head"), check_vma=False
    )
```

```python
import math

import jax
import jax.numpy as jnp
from jax import lax
from jax.experimental import pallas as pl
from jax.experimental.pallas import tpu as pltpu
from jax.sharding import PartitionSpec as P


WIDE = jnp.float32
NARROW = jnp.bfloat16
MASKED = -1e30
LAST_PIECES, LAST_GROUPS = 4, 2
SETTLE_PIECES, SETTLE_GROUPS = 4, 2
OWN_PIECES, NEAR_PIECES = 1, 2


def halves(x):
    top = x.astype(NARROW)
    return top, (x - top.astype(WIDE)).astype(NARROW)


def dot(a, b):
    return jnp.dot(a, b, preferred_element_type=WIDE)


def dot3(a, b):
    a_top, a_low = a
    b_top, b_low = b
    return dot(
        jnp.concatenate([a_top, a_low, a_top], axis=1),
        jnp.concatenate([b_top, b_top, b_low], axis=0),
    )


def whole(full_ref, own, other, parity):
    half = own.shape[0]
    full_ref[pl.ds(parity * half, half), :] = own
    full_ref[pl.ds((1 - parity) * half, half), :] = other
    return full_ref[...]


def invert(own_ref, other_ref, small_ref, inverse_ref, across_ref, dirs_ref, coef_ref, full_ref):
    length = own_ref.shape[1]
    place = lax.axis_index("head")
    parity = place % 2
    dirs_t = whole(full_ref, own_ref[...], other_ref[...], parity)
    across_ref[...] = dirs_t
    dirs_wide = dirs_t.astype(WIDE)
    dirs = dirs_wide.T.astype(NARROW)
    dirs_ref[...] = dirs
    power = jnp.sum(dirs_wide * dirs_wide, axis=0, keepdims=True) + 1e-06
    coef = small_ref[pl.ds(place // 2, 1), :] / power
    coef_ref[...] = jnp.broadcast_to(coef, coef_ref.shape)

    row = lax.broadcasted_iota(jnp.int32, (length, length), 0)
    col = lax.broadcasted_iota(jnp.int32, (length, length), 1)
    below = jnp.where(row > col, dot(dirs, dirs_t) * coef, 0.0)

    pair = jnp.where((row ^ col) == 1, -below, 0.0)
    joint = jnp.where((row // 2) ^ (col // 2) == 1, below, 0.0)
    joint = joint + jnp.sum(pair, axis=1, keepdims=True) * pltpu.roll(joint, 1, 0)
    joint = joint + pltpu.roll(joint, length - 1, 1) * jnp.sum(pair, axis=0, keepdims=True)
    inverse = jnp.where(row == col, 1.0, 0.0) + pair - joint
    block = 4
    while block < length:
        joint = halves(jnp.where((row // block) ^ (col // block) == 1, below, 0.0))
        parts = halves(inverse)
        step = block if block % 8 == 0 else length
        starts = range(step % length, length, 2 * step)
        lower = [jnp.concatenate([p[s : s + step] for s in starts], axis=0) for p in parts]
        change = dot3(halves(dot3(lower, joint)), parts)
        if step == length:
            inverse = inverse - change
        else:
            rows = []
            for at, start in enumerate(starts):
                rows.append(inverse[start - step : start])
                rows.append(inverse[start : start + step] - change[at * step : (at + 1) * step])
            inverse = jnp.concatenate(rows, axis=0)
        block *= 2
    inverse_ref[0], inverse_ref[1] = halves(inverse)


def prepare(
    own_ref, other_ref, inverse_ref, across_ref, dirs_ref, coef_ref,
    pack_ref, solved_ref, sides_ref, full_ref,
):
    half, length = own_ref.shape[0] // 2, own_ref.shape[1]
    width = 2 * half
    parity = lax.axis_index("head") % 2
    keys_t = whole(full_ref.at[0], own_ref[:half, :], other_ref[:half, :], parity)
    values_t = whole(full_ref.at[1], own_ref[half:, :], other_ref[half:, :], parity)
    dirs_t, dirs = across_ref[...], dirs_ref[...]
    row = lax.broadcasted_iota(jnp.int32, (length, length), 0)
    col = lax.broadcasted_iota(jnp.int32, (length, length), 1)
    top, low = inverse_ref[0], inverse_ref[1]
    reach_top, reach_low = halves(jnp.where(row > col, dot(dirs, keys_t), 0.0))
    right = jnp.concatenate([reach_top, dirs], axis=1)
    solved = dot(jnp.concatenate([top, low], axis=1), jnp.concatenate([right, right], axis=0))
    solved_reach = solved[:, :length] + dot(top, reach_low)
    solved_parts = halves(jnp.concatenate([solved_reach, solved[:, length:]], axis=1))
    change = dot3(halves(dirs_t.astype(WIDE) * coef_ref[:1, :]), solved_parts)
    pack_ref[:, :length] = (keys_t.astype(WIDE) - change[:, :length]).astype(NARROW)
    row_w = lax.broadcasted_iota(jnp.int32, (width, width), 0)
    col_w = lax.broadcasted_iota(jnp.int32, (width, width), 1)
    unit = jnp.where(row_w == col_w, 1.0, 0.0)
    pack_ref[:, length : length + width] = (unit - change[:, length:]).astype(NARROW)
    pack_ref[:, length + width :] = values_t.astype(WIDE).T.astype(NARROW)
    solved_ref[0] = solved_parts[0]
    solved_ref[1] = solved_parts[1]
    sides_ref[...] = jnp.concatenate([dirs_t, keys_t], axis=1)


def own_segment(
    queries_ref, solved_ref, sides_ref, coef_ref, pack_ref, moved_ref, peak_ref, sum_ref, mix_ref
):
    length = queries_ref.shape[0]
    width = sides_ref.shape[0]
    top, low = solved_ref[0], solved_ref[1]
    right = jnp.concatenate([top, top, low], axis=0)
    values = counted(pack_ref[:, length + width :])
    for part in pieces(moved_ref.shape[0], OWN_PIECES):
        heads = range(part.start // length, (part.start + part.size) // length)
        query = jnp.concatenate([queries_ref[:, pl.ds(h * width, width)] for h in heads], axis=0)
        row = lax.broadcasted_iota(jnp.int32, (part.size, length), 0) % length
        col = lax.broadcasted_iota(jnp.int32, (part.size, length), 1)
        past = row >= col
        plain = dot(query, sides_ref[...])
        met_top, met_low = halves(jnp.where(past, plain[:, :length] * coef_ref[:1, :], 0.0))
        change = dot(jnp.concatenate([met_top, met_low, met_top], axis=1), right)
        moved_ref[part, :] = (query.astype(WIDE) - change[:, length:]).astype(NARROW)
        scores = jnp.where(past, plain[:, length:] - change[:, :length], MASKED)
        peak = jnp.max(scores, axis=1, keepdims=True)
        mixed = dot(powers(scores, peak, width).astype(NARROW), values)
        peak_ref[part, :] = jnp.broadcast_to(peak, (part.size, width))
        mix_ref[part, :] = mixed[:, :width]
        sum_ref[part, :] = mixed[:, width:]


def counted(values):
    return jnp.concatenate([values, jnp.ones_like(values)], axis=1)


def powers(scores, peak, width):
    return jnp.exp2((scores - peak) * (width ** (-0.5) * math.log2(math.e)))


def carry(travel, block, length):
    both = dot(jnp.concatenate(halves(travel), axis=1), jnp.concatenate([block, block], axis=0))
    return both[:, :length].astype(NARROW), both[:, length:]


def gather(refs, core, keys_ref, values_ref, travel, length):
    width = keys_ref.shape[0]
    for slot, ref in enumerate(refs):
        if isinstance(ref, tuple):
            block = jnp.where(core == 1, ref[0][...], ref[1][...])
        else:
            block = ref[...]
        at = pl.ds(slot * length, length)
        values_ref[at, :] = counted(block[:, length + width :])
        block = block[:, : length + width]
        if travel is None:
            keys_ref[:, at] = block[:, :length]
            row = lax.broadcasted_iota(jnp.int32, (width, width), 0)
            col = lax.broadcasted_iota(jnp.int32, (width, width), 1)
            unit = jnp.where(row == col, 1.0, 0.0)
            travel = jnp.where(core == 1, block[:, length:].astype(WIDE), unit)
        else:
            keys_ref[:, at], travel = carry(travel, block, length)
    return travel


def pairs_of(far):
    order = []
    for straight, crossed in zip(far[::2], far[1::2]):
        order += [(straight, crossed), (crossed, straight)]
    return order


def take_in(query, keys, values, limits, peak, total, mix):
    width = mix.shape[1]
    scores = dot(query, keys)
    if limits is not None:
        column = lax.broadcasted_iota(jnp.int32, scores.shape, 1)
        scores = jnp.where((column >= limits[0]) & (column < limits[1]), scores, MASKED)
    above = jnp.maximum(peak, jnp.max(scores, axis=1, keepdims=True))
    fade = powers(peak, above, width)
    level = jnp.concatenate([above] * (scores.shape[1] // width), axis=1)
    mixed = dot(powers(scores, level, width).astype(NARROW), values)
    return above, total * fade + mixed[:, width:], mix * fade + mixed[:, :width]


def pieces(rows, count):
    size = rows // count
    return [pl.ds(start, size) for start in range(0, rows, size)]


def settle(out_ref, done_ref, sem, gain, parts, groups, states):
    length, width = out_ref.shape[0], gain.shape[1]

    def out_copy(head):
        cols = pl.ds(head * width, width)
        return pltpu.make_async_copy(done_ref.at[:, cols], out_ref.at[:, cols], sem.at[head])

    group = len(parts) // groups
    for at in range(0, len(parts), group):
        for part in parts[at : at + group]:
            total, mix = states(part)
            square = jnp.mean(mix * mix, axis=1, keepdims=True)
            strength = lax.rsqrt(square + 1e-06 * (total * total))
            normed = (mix * strength * gain).astype(NARROW)
            for start in range(0, part.size, length):
                head = (part.start + start) // length
                done_ref[:, pl.ds(head * width, width)] = normed[start : start + length]
        first = parts[at].start // length
        for head in range(first, first + group * parts[at].size // length):
            out_copy(head).start()
    for head in range(out_ref.shape[1] // width):
        out_copy(head).wait()


def update(moved_ref, olds, news, keys, values, limits):
    for part in pieces(moved_ref.shape[0], NEAR_PIECES):
        fresh = take_in(
            moved_ref[part, :], keys, values, limits, *(old[part, :] for old in olds)
        )
        for new, value in zip(news, fresh):
            new[part, :] = value


def attend_near(
    moved_ref, peak_ref, sum_ref, mix_ref, small_ref, mate_ref, straight_ref, crossed_ref,
    peak_out, sum_out, mix_out, travel_out, out_ref, keys_ref, values_ref, done_ref, sem,
):
    length = out_ref.shape[0]
    place = lax.axis_index("seq")
    core, chip_place = place % 2, place // 2
    olds, news = (peak_ref, sum_ref, mix_ref), (peak_out, sum_out, mix_out)

    @pl.when(chip_place > 0)
    def _():
        order = [mate_ref] + pairs_of([straight_ref, crossed_ref])
        travel_out[...] = gather(order, core, keys_ref, values_ref, None, length)
        limits = ((1 - core) * length, 3 * length)
        update(moved_ref, olds, news, keys_ref[...], values_ref[...], limits)

    @pl.when((chip_place == 0) & (core == 1))
    def _():
        span = pl.ds(0, length)
        gather([mate_ref], core, keys_ref, values_ref, None, length)
        update(moved_ref, olds, news, keys_ref[:, span], values_ref[span, :], None)

    @pl.when(chip_place == 0)
    def _():
        parts = pieces(moved_ref.shape[0], SETTLE_PIECES)
        states = lambda part: (sum_out[part, :], mix_out[part, :])
        settle(out_ref, done_ref, sem, small_ref[small_ref.shape[0] - 1 :, :], parts, SETTLE_GROUPS, states)


def attend_next(
    moved_ref, peak_ref, sum_ref, mix_ref, travel_ref, out_in, small_ref, straight_ref, crossed_ref,
    peak_out, sum_out, mix_out, travel_out, out_ref, keys_ref, values_ref, done_ref, sem,
):
    length = out_ref.shape[0]
    place = lax.axis_index("seq")
    chip_place = place // 2
    olds, news = (peak_ref, sum_ref, mix_ref), (peak_out, sum_out, mix_out)

    @pl.when(chip_place > 1)
    def _():
        order = pairs_of([straight_ref, crossed_ref])
        travel_out[...] = gather(order, place % 2, keys_ref, values_ref, travel_ref[...], length)
        update(moved_ref, olds, news, keys_ref[...], values_ref[...], None)

    @pl.when((chip_place == 1) | (chip_place == 2))
    def _():
        parts = pieces(moved_ref.shape[0], SETTLE_PIECES)
        states = lambda part: (sum_out[part, :], mix_out[part, :])
        settle(out_ref, done_ref, sem, small_ref[small_ref.shape[0] - 1 :, :], parts, SETTLE_GROUPS, states)


def attend_last(*refs):
    moved_ref, peak_ref, sum_ref, mix_ref, travel_ref, _, small_ref = refs[:7]
    out_ref, keys_ref, values_ref, done_ref, sem = refs[-5:]
    far = refs[7:-5]
    length = out_ref.shape[0]
    place = lax.axis_index("seq")
    core, chip_place = place % 2, place // 2

    @pl.when(chip_place > 2)
    def _():
        gather(pairs_of(far), core, keys_ref, values_ref, travel_ref[...], length)
        limits = (0, 2 * (chip_place - 2) * length) if len(far) > 2 else None
        parts = pieces(moved_ref.shape[0], LAST_PIECES)
        states = lambda part: take_in(
            moved_ref[part, :], keys_ref[...], values_ref[...], limits,
            peak_ref[part, :], sum_ref[part, :], mix_ref[part, :],
        )[1:]
        settle(out_ref, done_ref, sem, small_ref[small_ref.shape[0] - 1 :, :], parts, LAST_GROUPS, states)


LOCAL = pl.BlockSpec(memory_space=pltpu.VMEM)
ANYWHERE = pl.BlockSpec(memory_space=pltpu.HBM)


def call(kernel, outs, count, scratch=(), flops=1e8, spots=None, aliases=None, places=None):
    return pl.pallas_call(
        kernel,
        out_shape=outs,
        in_specs=places or [LOCAL] * count,
        out_specs=spots or jax.tree.map(lambda _: LOCAL, outs),
        scratch_shapes=list(scratch),
        input_output_aliases=aliases or {},
        compiler_params=pltpu.CompilerParams(vmem_limit_bytes=16 << 20),
        cost_estimate=pl.CostEstimate(
            flops=int(flops), bytes_accessed=1 << 20, transcendentals=1 << 17
        ),
    )


def shards(queries, keys, values, directions, beta, gain):
    length, half = directions.shape
    width = 2 * half
    heads = queries.shape[1] // width
    segments = lax.axis_size("seq")
    places = range(lax.axis_size("head"))

    def partner(block):
        return lax.ppermute(block, "head", [(place, place ^ 1) for place in places])

    other_dirs = partner(directions.T)
    own = jnp.concatenate([keys.T, values.T], axis=0)
    other = partner(own)
    shape = jax.ShapeDtypeStruct
    small = jnp.concatenate([beta.T, gain.reshape(1, -1)], axis=0)
    square = shape((width, length), NARROW)
    inverse, dirs_t, dirs, coef = call(
        invert,
        (shape((2, length, length), NARROW), square, square, shape((8, length), WIDE)),
        3,
        [pltpu.VMEM((width, length), NARROW)],
    )(directions.T, other_dirs, small)
    pack, solved, sides = call(
        prepare,
        (
            shape((width, 2 * length + width), NARROW),
            shape((2, length, length + width), NARROW),
            shape((width, 2 * length), NARROW),
        ),
        6,
        [pltpu.VMEM((2, width, length), NARROW)],
    )(own, other, inverse, dirs_t, dirs, coef)

    def across(block, first=0):
        return lax.ppermute(block, "seq", [(i, i ^ 1) for i in range(2 * first, segments)])

    mate = across(pack)
    chips = segments // 2
    far = []
    for chip in range(1, chips):
        pairs = [(i, (i + 2 * chip) % segments) for i in range(segments)]
        far.append(lax.ppermute(pack, "seq", pairs))
    state_shape = (shape((heads * length, width), WIDE),) * 3
    moved, *state = call(
        own_segment, (shape((heads * length, width), NARROW),) + state_shape, 5
    )(queries, solved, sides, coef, pack)

    def stores(count):
        return [
            pltpu.VMEM((width, count * length), NARROW),
            pltpu.VMEM((count * length, 2 * width), NARROW),
        ]

    crossed = across(far[0])
    states = state_shape + (shape((width, width), WIDE), shape((length, heads * width), NARROW))
    spots = (LOCAL,) * 4 + (ANYWHERE,)
    ends = [pltpu.VMEM((length, heads * width), NARROW), pltpu.SemaphoreType.DMA((heads,))]
    in_place = {1: 0, 2: 1, 3: 2}
    *state, travel, out = call(
        attend_near, states, 8, stores(3) + ends, spots=spots, aliases=in_place
    )(moved, *state, small, mate, far[0], crossed)
    places = [ANYWHERE if at == 5 else LOCAL for at in range(9)]
    crossed = across(far[1])
    *state, travel, out = call(
        attend_next,
        states,
        9,
        stores(2) + ends,
        spots=spots,
        aliases={**in_place, 4: 3, 5: 4},
        places=places,
    )(moved, *state, travel, out, small, far[1], crossed)
    blocks = []
    for chip in range(3, chips):
        blocks += [far[chip - 1], across(far[chip - 1])]
    count = 7 + len(blocks)
    return call(
        attend_last,
        shape((length, heads * width), NARROW),
        count,
        stores(2 * (chips - 3)) + ends,
        flops=1e9,
        spots=ANYWHERE,
        aliases={5: 0},
        places=[ANYWHERE if at == 5 else LOCAL for at in range(count)],
    )(moved, *state, travel, out, small, *blocks)


def solution(mesh):
    placed = (
        P("seq", "head"),
        P("seq", "head"),
        P("seq", "head"),
        P("seq", "head"),
        P("seq", None),
        P(),
    )

    return jax.shard_map(
        shards, mesh=mesh, in_specs=placed, out_specs=P("seq", "head"), check_vma=False
    )
```

```python
import math

import jax
import jax.numpy as jnp
from jax import lax
from jax.experimental import pallas as pl
from jax.experimental.pallas import tpu as pltpu
from jax.sharding import PartitionSpec as P


WIDE = jnp.float32
NARROW = jnp.bfloat16
MASKED = -1e30
LAST_PIECES, LAST_GROUPS = 4, 2
SETTLE_PIECES, SETTLE_GROUPS = 4, 2
OWN_PIECES, NEAR_PIECES = 1, 2


def halves(x):
    top = x.astype(NARROW)
    return top, (x - top.astype(WIDE)).astype(NARROW)


def dot(a, b):
    return jnp.dot(a, b, preferred_element_type=WIDE)


def dot3(a, b):
    a_top, a_low = a
    b_top, b_low = b
    return dot(
        jnp.concatenate([a_top, a_low, a_top], axis=1),
        jnp.concatenate([b_top, b_top, b_low], axis=0),
    )


def whole(full_ref, own, other, parity):
    half = own.shape[0]
    full_ref[pl.ds(parity * half, half), :] = own
    full_ref[pl.ds((1 - parity) * half, half), :] = other
    return full_ref[...]


def invert(own_ref, other_ref, small_ref, inverse_ref, across_ref, dirs_ref, coef_ref, full_ref):
    length = own_ref.shape[1]
    place = lax.axis_index("head")
    parity = place % 2
    dirs_t = whole(full_ref, own_ref[...], other_ref[...], parity)
    across_ref[...] = dirs_t
    dirs_wide = dirs_t.astype(WIDE)
    dirs = dirs_wide.T.astype(NARROW)
    dirs_ref[...] = dirs
    power = jnp.sum(dirs_wide * dirs_wide, axis=0, keepdims=True) + 1e-06
    coef = small_ref[pl.ds(place // 2, 1), :] / power
    coef_ref[...] = jnp.broadcast_to(coef, coef_ref.shape)

    row = lax.broadcasted_iota(jnp.int32, (length, length), 0)
    col = lax.broadcasted_iota(jnp.int32, (length, length), 1)
    below = jnp.where(row > col, dot(dirs, dirs_t) * coef, 0.0)

    pair = jnp.where((row ^ col) == 1, -below, 0.0)
    joint = jnp.where((row // 2) ^ (col // 2) == 1, below, 0.0)
    joint = joint + jnp.sum(pair, axis=1, keepdims=True) * pltpu.roll(joint, 1, 0)
    joint = joint + pltpu.roll(joint, length - 1, 1) * jnp.sum(pair, axis=0, keepdims=True)
    inverse = jnp.where(row == col, 1.0, 0.0) + pair - joint
    block = 4
    while block < length:
        joint = halves(jnp.where((row // block) ^ (col // block) == 1, below, 0.0))
        parts = halves(inverse)
        step = block if block % 8 == 0 else length
        starts = range(step % length, length, 2 * step)
        lower = [jnp.concatenate([p[s : s + step] for s in starts], axis=0) for p in parts]
        change = dot3(halves(dot3(lower, joint)), parts)
        if step == length:
            inverse = inverse - change
        else:
            rows = []
            for at, start in enumerate(starts):
                rows.append(inverse[start - step : start])
                rows.append(inverse[start : start + step] - change[at * step : (at + 1) * step])
            inverse = jnp.concatenate(rows, axis=0)
        block *= 2
    inverse_ref[0], inverse_ref[1] = halves(inverse)


def prepare(
    own_ref, other_ref, inverse_ref, across_ref, dirs_ref, coef_ref,
    pack_ref, solved_ref, sides_ref, full_ref,
):
    half, length = own_ref.shape[0] // 2, own_ref.shape[1]
    width = 2 * half
    parity = lax.axis_index("head") % 2
    keys_t = whole(full_ref.at[0], own_ref[:half, :], other_ref[:half, :], parity)
    values_t = whole(full_ref.at[1], own_ref[half:, :], other_ref[half:, :], parity)
    dirs_t, dirs = across_ref[...], dirs_ref[...]
    row = lax.broadcasted_iota(jnp.int32, (length, length), 0)
    col = lax.broadcasted_iota(jnp.int32, (length, length), 1)
    top, low = inverse_ref[0], inverse_ref[1]
    reach_top, reach_low = halves(jnp.where(row > col, dot(dirs, keys_t), 0.0))
    right = jnp.concatenate([reach_top, dirs], axis=1)
    solved = dot(jnp.concatenate([top, low], axis=1), jnp.concatenate([right, right], axis=0))
    solved_reach = solved[:, :length] + dot(top, reach_low)
    solved_parts = halves(jnp.concatenate([solved_reach, solved[:, length:]], axis=1))
    change = dot3(halves(dirs_t.astype(WIDE) * coef_ref[:1, :]), solved_parts)
    pack_ref[:, :length] = (keys_t.astype(WIDE) - change[:, :length]).astype(NARROW)
    row_w = lax.broadcasted_iota(jnp.int32, (width, width), 0)
    col_w = lax.broadcasted_iota(jnp.int32, (width, width), 1)
    unit = jnp.where(row_w == col_w, 1.0, 0.0)
    pack_ref[:, length : length + width] = (unit - change[:, length:]).astype(NARROW)
    pack_ref[:, length + width :] = values_t.astype(WIDE).T.astype(NARROW)
    solved_ref[0] = solved_parts[0]
    solved_ref[1] = solved_parts[1]
    sides_ref[...] = jnp.concatenate([dirs_t, keys_t], axis=1)


def own_segment(
    queries_ref, solved_ref, sides_ref, coef_ref, pack_ref, moved_ref, peak_ref, sum_ref, mix_ref
):
    length = queries_ref.shape[0]
    width = sides_ref.shape[0]
    top, low = solved_ref[0], solved_ref[1]
    right = jnp.concatenate([top, top, low], axis=0)
    values = counted(pack_ref[:, length + width :])
    for part in pieces(moved_ref.shape[0], OWN_PIECES):
        heads = range(part.start // length, (part.start + part.size) // length)
        query = jnp.concatenate([queries_ref[:, pl.ds(h * width, width)] for h in heads], axis=0)
        row = lax.broadcasted_iota(jnp.int32, (part.size, length), 0) % length
        col = lax.broadcasted_iota(jnp.int32, (part.size, length), 1)
        past = row >= col
        plain = dot(query, sides_ref[...])
        met_top, met_low = halves(jnp.where(past, plain[:, :length] * coef_ref[:1, :], 0.0))
        change = dot(jnp.concatenate([met_top, met_low, met_top], axis=1), right)
        moved_ref[part, :] = (query.astype(WIDE) - change[:, length:]).astype(NARROW)
        scores = jnp.where(past, plain[:, length:] - change[:, :length], MASKED)
        peak = jnp.max(scores, axis=1, keepdims=True)
        mixed = dot(powers(scores, peak, width).astype(NARROW), values)
        peak_ref[part, :] = jnp.broadcast_to(peak, (part.size, width))
        mix_ref[part, :] = mixed[:, :width]
        sum_ref[part, :] = mixed[:, width:]


def counted(values):
    return jnp.concatenate([values, jnp.ones_like(values)], axis=1)


def powers(scores, peak, width):
    return jnp.exp2((scores - peak) * (width ** (-0.5) * math.log2(math.e)))


def carry(travel, block, length):
    both = dot(jnp.concatenate(halves(travel), axis=1), jnp.concatenate([block, block], axis=0))
    return both[:, :length].astype(NARROW), both[:, length:]


def gather(refs, core, keys_ref, values_ref, travel, length):
    width = keys_ref.shape[0]
    for slot, ref in enumerate(refs):
        if isinstance(ref, tuple):
            block = jnp.where(core == 1, ref[0][...], ref[1][...])
        else:
            block = ref[...]
        at = pl.ds(slot * length, length)
        values_ref[at, :] = counted(block[:, length + width :])
        block = block[:, : length + width]
        if travel is None:
            keys_ref[:, at] = block[:, :length]
            row = lax.broadcasted_iota(jnp.int32, (width, width), 0)
            col = lax.broadcasted_iota(jnp.int32, (width, width), 1)
            unit = jnp.where(row == col, 1.0, 0.0)
            travel = jnp.where(core == 1, block[:, length:].astype(WIDE), unit)
        else:
            keys_ref[:, at], travel = carry(travel, block, length)
    return travel


def pairs_of(far):
    order = []
    for straight, crossed in zip(far[::2], far[1::2]):
        order += [(straight, crossed), (crossed, straight)]
    return order


def take_in(query, keys, values, limits, peak, total, mix):
    width = mix.shape[1]
    scores = dot(query, keys)
    if limits is not None:
        column = lax.broadcasted_iota(jnp.int32, scores.shape, 1)
        scores = jnp.where((column >= limits[0]) & (column < limits[1]), scores, MASKED)
    above = jnp.maximum(peak, jnp.max(scores, axis=1, keepdims=True))
    fade = powers(peak, above, width)
    level = jnp.concatenate([above] * (scores.shape[1] // width), axis=1)
    mixed = dot(powers(scores, level, width).astype(NARROW), values)
    return above, total * fade + mixed[:, width:], mix * fade + mixed[:, :width]


def pieces(rows, count):
    size = rows // count
    return [pl.ds(start, size) for start in range(0, rows, size)]


def settle(out_ref, done_ref, sem, gain, parts, groups, states):
    length, width = out_ref.shape[0], gain.shape[1]

    def out_copy(head):
        cols = pl.ds(head * width, width)
        return pltpu.make_async_copy(done_ref.at[:, cols], out_ref.at[:, cols], sem.at[head])

    group = len(parts) // groups
    for at in range(0, len(parts), group):
        for part in parts[at : at + group]:
            total, mix = states(part)
            square = jnp.mean(mix * mix, axis=1, keepdims=True)
            strength = lax.rsqrt(square + 1e-06 * (total * total))
            normed = (mix * strength * gain).astype(NARROW)
            for start in range(0, part.size, length):
                head = (part.start + start) // length
                done_ref[:, pl.ds(head * width, width)] = normed[start : start + length]
        first = parts[at].start // length
        for head in range(first, first + group * parts[at].size // length):
            out_copy(head).start()
    for head in range(out_ref.shape[1] // width):
        out_copy(head).wait()


def update(moved_ref, olds, news, keys, values, limits):
    for part in pieces(moved_ref.shape[0], NEAR_PIECES):
        fresh = take_in(
            moved_ref[part, :], keys, values, limits, *(old[part, :] for old in olds)
        )
        for new, value in zip(news, fresh):
            new[part, :] = value


def ready(pack_ref, mate_ref, ready_ref):
    width = pack_ref.shape[0]
    length = pack_ref.shape[1] - 2 * width
    keys = pack_ref[:, :length]
    through = dot(mate_ref[:, pl.ds(length, width)], keys).astype(NARROW)
    ready_ref[:, :length] = jnp.where(lax.axis_index("seq") % 2 == 0, through, keys)
    ready_ref[:, length:] = pack_ref[:, length + width :]


def attend_near(
    moved_ref, peak_ref, sum_ref, mix_ref, small_ref, mate_ref, straight_ref, crossed_ref,
    peak_out, sum_out, mix_out, travel_out, out_ref, keys_ref, values_ref, done_ref, sem,
):
    length = out_ref.shape[0]
    place = lax.axis_index("seq")
    core, chip_place = place % 2, place // 2
    olds, news = (peak_ref, sum_ref, mix_ref), (peak_out, sum_out, mix_out)

    @pl.when(chip_place > 0)
    def _():
        order = [mate_ref] + pairs_of([straight_ref, crossed_ref])
        travel_out[...] = gather(order, core, keys_ref, values_ref, None, length)
        limits = ((1 - core) * length, 3 * length)
        update(moved_ref, olds, news, keys_ref[...], values_ref[...], limits)

    @pl.when((chip_place == 0) & (core == 1))
    def _():
        span = pl.ds(0, length)
        gather([mate_ref], core, keys_ref, values_ref, None, length)
        update(moved_ref, olds, news, keys_ref[:, span], values_ref[span, :], None)

    @pl.when(chip_place == 0)
    def _():
        parts = pieces(moved_ref.shape[0], SETTLE_PIECES)
        states = lambda part: (sum_out[part, :], mix_out[part, :])
        settle(out_ref, done_ref, sem, small_ref[small_ref.shape[0] - 1 :, :], parts, SETTLE_GROUPS, states)


def attend_next(
    moved_ref, peak_ref, sum_ref, mix_ref, travel_ref, out_in, small_ref, straight_ref, crossed_ref,
    peak_out, sum_out, mix_out, travel_out, out_ref, keys_ref, values_ref, done_ref, sem,
):
    length = out_ref.shape[0]
    place = lax.axis_index("seq")
    chip_place = place // 2
    olds, news = (peak_ref, sum_ref, mix_ref), (peak_out, sum_out, mix_out)

    @pl.when(chip_place > 1)
    def _():
        order = pairs_of([straight_ref, crossed_ref])
        travel_out[...] = gather(order, place % 2, keys_ref, values_ref, travel_ref[...], length)
        update(moved_ref, olds, news, keys_ref[...], values_ref[...], None)

    @pl.when((chip_place == 1) | (chip_place == 2))
    def _():
        parts = pieces(moved_ref.shape[0], SETTLE_PIECES)
        states = lambda part: (sum_out[part, :], mix_out[part, :])
        settle(out_ref, done_ref, sem, small_ref[small_ref.shape[0] - 1 :, :], parts, SETTLE_GROUPS, states)


def attend_last(*refs):
    moved_ref, peak_ref, sum_ref, mix_ref, travel_ref, _, small_ref = refs[:7]
    out_ref, keys_ref, values_ref, done_ref, sem = refs[-5:]
    far = refs[7:-5]
    length = out_ref.shape[0]
    place = lax.axis_index("seq")
    core, chip_place = place % 2, place // 2

    @pl.when(chip_place > 2)
    def _():
        order = pairs_of(far[:-2])
        travel = gather(order, core, keys_ref, values_ref, travel_ref[...], length)
        straight, crossed = far[-2][...], far[-1][...]
        pair = [jnp.where(core == 1, straight, crossed), jnp.where(core == 1, crossed, straight)]
        keys = jnp.concatenate([block[:, :length] for block in pair], axis=1)
        keys = dot(jnp.concatenate(halves(travel), axis=1), jnp.concatenate([keys, keys], axis=0))
        keys_ref[:, pl.ds(len(order) * length, 2 * length)] = keys.astype(NARROW)
        for slot, block in enumerate(pair, len(order)):
            values_ref[pl.ds(slot * length, length), :] = counted(block[:, length:])
        limits = (0, 2 * (chip_place - 2) * length) if order else None
        parts = pieces(moved_ref.shape[0], LAST_PIECES)
        states = lambda part: take_in(
            moved_ref[part, :], keys_ref[...], values_ref[...], limits,
            peak_ref[part, :], sum_ref[part, :], mix_ref[part, :],
        )[1:]
        settle(out_ref, done_ref, sem, small_ref[small_ref.shape[0] - 1 :, :], parts, LAST_GROUPS, states)


LOCAL = pl.BlockSpec(memory_space=pltpu.VMEM)
ANYWHERE = pl.BlockSpec(memory_space=pltpu.HBM)


def call(kernel, outs, count, scratch=(), flops=1e8, spots=None, aliases=None, places=None):
    return pl.pallas_call(
        kernel,
        out_shape=outs,
        in_specs=places or [LOCAL] * count,
        out_specs=spots or jax.tree.map(lambda _: LOCAL, outs),
        scratch_shapes=list(scratch),
        input_output_aliases=aliases or {},
        compiler_params=pltpu.CompilerParams(vmem_limit_bytes=16 << 20),
        cost_estimate=pl.CostEstimate(
            flops=int(flops), bytes_accessed=1 << 20, transcendentals=1 << 17
        ),
    )


def shards(queries, keys, values, directions, beta, gain):
    length, half = directions.shape
    width = 2 * half
    heads = queries.shape[1] // width
    segments = lax.axis_size("seq")
    places = range(lax.axis_size("head"))

    def partner(block):
        return lax.ppermute(block, "head", [(place, place ^ 1) for place in places])

    other_dirs = partner(directions.T)
    own = jnp.concatenate([keys.T, values.T], axis=0)
    other = partner(own)
    shape = jax.ShapeDtypeStruct
    small = jnp.concatenate([beta.T, gain.reshape(1, -1)], axis=0)
    square = shape((width, length), NARROW)
    inverse, dirs_t, dirs, coef = call(
        invert,
        (shape((2, length, length), NARROW), square, square, shape((8, length), WIDE)),
        3,
        [pltpu.VMEM((width, length), NARROW)],
    )(directions.T, other_dirs, small)
    pack, solved, sides = call(
        prepare,
        (
            shape((width, 2 * length + width), NARROW),
            shape((2, length, length + width), NARROW),
            shape((width, 2 * length), NARROW),
        ),
        6,
        [pltpu.VMEM((2, width, length), NARROW)],
    )(own, other, inverse, dirs_t, dirs, coef)

    def across(block, first=0):
        return lax.ppermute(block, "seq", [(i, i ^ 1) for i in range(2 * first, segments)])

    mate = across(pack)
    chips = segments // 2
    far = []
    for chip in range(1, chips):
        pairs = [(i, (i + 2 * chip) % segments) for i in range(segments)]
        block = pack
        if chip == chips - 1:
            block = call(ready, shape((width, length + width), NARROW), 2)(pack, mate)
        far.append(lax.ppermute(block, "seq", pairs))
    state_shape = (shape((heads * length, width), WIDE),) * 3
    moved, *state = call(
        own_segment, (shape((heads * length, width), NARROW),) + state_shape, 5
    )(queries, solved, sides, coef, pack)

    def stores(count):
        return [
            pltpu.VMEM((width, count * length), NARROW),
            pltpu.VMEM((count * length, 2 * width), NARROW),
        ]

    crossed = across(far[0])
    states = state_shape + (shape((width, width), WIDE), shape((length, heads * width), NARROW))
    spots = (LOCAL,) * 4 + (ANYWHERE,)
    ends = [pltpu.VMEM((length, heads * width), NARROW), pltpu.SemaphoreType.DMA((heads,))]
    in_place = {1: 0, 2: 1, 3: 2}
    *state, travel, out = call(
        attend_near, states, 8, stores(3) + ends, spots=spots, aliases=in_place
    )(moved, *state, small, mate, far[0], crossed)
    places = [ANYWHERE if at == 5 else LOCAL for at in range(9)]
    crossed = across(far[1])
    *state, travel, out = call(
        attend_next,
        states,
        9,
        stores(2) + ends,
        spots=spots,
        aliases={**in_place, 4: 3, 5: 4},
        places=places,
    )(moved, *state, travel, out, small, far[1], crossed)
    blocks = []
    for chip in range(3, chips):
        blocks += [far[chip - 1], across(far[chip - 1])]
    count = 7 + len(blocks)
    return call(
        attend_last,
        shape((length, heads * width), NARROW),
        count,
        stores(2 * (chips - 3)) + ends,
        flops=1e9,
        spots=ANYWHERE,
        aliases={5: 0},
        places=[ANYWHERE if at == 5 else LOCAL for at in range(count)],
    )(moved, *state, travel, out, small, *blocks)


def solution(mesh):
    placed = (
        P("seq", "head"),
        P("seq", "head"),
        P("seq", "head"),
        P("seq", "head"),
        P("seq", None),
        P(),
    )

    return jax.shard_map(
        shards, mesh=mesh, in_specs=placed, out_specs=P("seq", "head"), check_vma=False
    )
```

```python
import math

import jax
import jax.numpy as jnp
from jax import lax
from jax.experimental import pallas as pl
from jax.experimental.pallas import tpu as pltpu
from jax.sharding import PartitionSpec as P


WIDE = jnp.float32
NARROW = jnp.bfloat16
MASKED = -1e30
LAST_PIECES, LAST_GROUPS = 8, 2
SETTLE_PIECES, SETTLE_GROUPS = 4, 2
OWN_PIECES, NEAR_PIECES = 1, 2


def halves(x):
    top = x.astype(NARROW)
    return top, (x - top.astype(WIDE)).astype(NARROW)


def dot(a, b):
    return jnp.dot(a, b, preferred_element_type=WIDE)


def dot3(a, b):
    a_top, a_low = a
    b_top, b_low = b
    return dot(
        jnp.concatenate([a_top, a_low, a_top], axis=1),
        jnp.concatenate([b_top, b_top, b_low], axis=0),
    )


def whole(full_ref, own, other, parity):
    half = own.shape[0]
    full_ref[pl.ds(parity * half, half), :] = own
    full_ref[pl.ds((1 - parity) * half, half), :] = other
    return full_ref[...]


def invert(
    own_ref, other_ref, small_ref,
    inverse_ref, across_ref, dirs_ref, coef_ref, spread_ref, transform_ref, full_ref,
):
    length = own_ref.shape[1]
    place = lax.axis_index("head")
    parity = place % 2
    dirs_t = whole(full_ref, own_ref[...], other_ref[...], parity)
    across_ref[...] = dirs_t
    dirs_wide = dirs_t.astype(WIDE)
    dirs = dirs_wide.T.astype(NARROW)
    dirs_ref[...] = dirs
    power = jnp.sum(dirs_wide * dirs_wide, axis=0, keepdims=True) + 1e-06
    coef = small_ref[pl.ds(place // 2, 1), :] / power
    coef_ref[...] = jnp.broadcast_to(coef, coef_ref.shape)

    row = lax.broadcasted_iota(jnp.int32, (length, length), 0)
    col = lax.broadcasted_iota(jnp.int32, (length, length), 1)
    below = jnp.where(row > col, dot(dirs, dirs_t) * coef, 0.0)

    pair = jnp.where((row ^ col) == 1, -below, 0.0)
    joint = jnp.where((row // 2) ^ (col // 2) == 1, below, 0.0)
    joint = joint + jnp.sum(pair, axis=1, keepdims=True) * pltpu.roll(joint, 1, 0)
    joint = joint + pltpu.roll(joint, length - 1, 1) * jnp.sum(pair, axis=0, keepdims=True)
    inverse = jnp.where(row == col, 1.0, 0.0) + pair - joint
    block = 4
    while block < length:
        joint = halves(jnp.where((row // block) ^ (col // block) == 1, below, 0.0))
        parts = halves(inverse)
        step = block if block % 8 == 0 else length
        starts = range(step % length, length, 2 * step)
        lower = [jnp.concatenate([p[s : s + step] for s in starts], axis=0) for p in parts]
        change = dot3(halves(dot3(lower, joint)), parts)
        if step == length:
            inverse = inverse - change
        else:
            rows = []
            for at, start in enumerate(starts):
                rows.append(inverse[start - step : start])
                rows.append(inverse[start : start + step] - change[at * step : (at + 1) * step])
            inverse = jnp.concatenate(rows, axis=0)
        block *= 2
    top, low = halves(inverse)
    inverse_ref[0], inverse_ref[1] = top, low
    spread = halves(
        dot(jnp.concatenate([top, low], axis=1), jnp.concatenate([dirs, dirs], axis=0))
    )
    spread_ref[0], spread_ref[1] = spread
    width = dirs_t.shape[0]
    row_w = lax.broadcasted_iota(jnp.int32, (width, width), 0)
    col_w = lax.broadcasted_iota(jnp.int32, (width, width), 1)
    unit = jnp.where(row_w == col_w, 1.0, 0.0)
    transform_ref[...] = (unit - dot3(halves(dirs_wide * coef), spread)).astype(NARROW)


def prepare(
    own_ref, other_ref, inverse_ref, across_ref, dirs_ref, coef_ref, spread_ref, transform_ref,
    pack_ref, solved_ref, sides_ref, full_ref,
):
    half, length = own_ref.shape[0] // 2, own_ref.shape[1]
    width = 2 * half
    parity = lax.axis_index("head") % 2
    keys_t = whole(full_ref.at[0], own_ref[:half, :], other_ref[:half, :], parity)
    values_t = whole(full_ref.at[1], own_ref[half:, :], other_ref[half:, :], parity)
    dirs_t, dirs = across_ref[...], dirs_ref[...]
    row = lax.broadcasted_iota(jnp.int32, (length, length), 0)
    col = lax.broadcasted_iota(jnp.int32, (length, length), 1)
    top, low = inverse_ref[0], inverse_ref[1]
    reach = halves(jnp.where(row > col, dot(dirs, keys_t), 0.0))
    solved = halves(dot3((top, low), reach))
    change = dot3(halves(dirs_t.astype(WIDE) * coef_ref[:1, :]), solved)
    pack_ref[:, :length] = (keys_t.astype(WIDE) - change).astype(NARROW)
    pack_ref[:, length : length + width] = transform_ref[...]
    pack_ref[:, length + width :] = values_t.astype(WIDE).T.astype(NARROW)
    for at in range(2):
        solved_ref[at] = jnp.concatenate([solved[at], spread_ref[at]], axis=1)
    sides_ref[...] = jnp.concatenate([dirs_t, keys_t], axis=1)


def own_segment(
    queries_ref, solved_ref, sides_ref, coef_ref, pack_ref, moved_ref, peak_ref, sum_ref, mix_ref
):
    length = queries_ref.shape[0]
    width = sides_ref.shape[0]
    top, low = solved_ref[0], solved_ref[1]
    right = jnp.concatenate([top, top, low], axis=0)
    values = counted(pack_ref[:, length + width :])
    for part in pieces(moved_ref.shape[0], OWN_PIECES):
        heads = range(part.start // length, (part.start + part.size) // length)
        query = jnp.concatenate([queries_ref[:, pl.ds(h * width, width)] for h in heads], axis=0)
        row = lax.broadcasted_iota(jnp.int32, (part.size, length), 0) % length
        col = lax.broadcasted_iota(jnp.int32, (part.size, length), 1)
        past = row >= col
        plain = dot(query, sides_ref[...])
        met_top, met_low = halves(jnp.where(past, plain[:, :length] * coef_ref[:1, :], 0.0))
        change = dot(jnp.concatenate([met_top, met_low, met_top], axis=1), right)
        moved_ref[part, :] = (query.astype(WIDE) - change[:, length:]).astype(NARROW)
        scores = jnp.where(past, plain[:, length:] - change[:, :length], MASKED)
        peak = jnp.max(scores, axis=1, keepdims=True)
        mixed = dot(powers(scores, peak, width).astype(NARROW), values)
        peak_ref[part, :] = jnp.broadcast_to(peak, (part.size, width))
        mix_ref[part, :] = mixed[:, :width]
        sum_ref[part, :] = mixed[:, width:]


def counted(values):
    return jnp.concatenate([values, jnp.ones_like(values)], axis=1)


def powers(scores, peak, width):
    return jnp.exp2((scores - peak) * (width ** (-0.5) * math.log2(math.e)))


def carry(travel, block, length):
    both = dot(jnp.concatenate(halves(travel), axis=1), jnp.concatenate([block, block], axis=0))
    return both[:, :length].astype(NARROW), both[:, length:]


def gather(refs, core, keys_ref, values_ref, travel, length):
    width = keys_ref.shape[0]
    for slot, ref in enumerate(refs):
        if isinstance(ref, tuple):
            block = jnp.where(core == 1, ref[0][...], ref[1][...])
        else:
            block = ref[...]
        at = pl.ds(slot * length, length)
        values_ref[at, :] = counted(block[:, length + width :])
        block = block[:, : length + width]
        if travel is None:
            keys_ref[:, at] = block[:, :length]
            row = lax.broadcasted_iota(jnp.int32, (width, width), 0)
            col = lax.broadcasted_iota(jnp.int32, (width, width), 1)
            unit = jnp.where(row == col, 1.0, 0.0)
            travel = jnp.where(core == 1, block[:, length:].astype(WIDE), unit)
        else:
            keys_ref[:, at], travel = carry(travel, block, length)
    return travel


def pairs_of(far):
    order = []
    for straight, crossed in zip(far[::2], far[1::2]):
        order += [(straight, crossed), (crossed, straight)]
    return order


def take_in(query, keys, values, limits, peak, total, mix):
    width = mix.shape[1]
    scores = dot(query, keys)
    if limits is not None:
        column = lax.broadcasted_iota(jnp.int32, scores.shape, 1)
        scores = jnp.where((column >= limits[0]) & (column < limits[1]), scores, MASKED)
    above = jnp.maximum(peak, jnp.max(scores, axis=1, keepdims=True))
    fade = powers(peak, above, width)
    level = jnp.concatenate([above] * (scores.shape[1] // width), axis=1)
    mixed = dot(powers(scores, level, width).astype(NARROW), values)
    return above, total * fade + mixed[:, width:], mix * fade + mixed[:, :width]


def pieces(rows, count):
    size = rows // count
    return [pl.ds(start, size) for start in range(0, rows, size)]


def settle(out_ref, done_ref, sem, gain, parts, groups, states):
    length, width = out_ref.shape[0], gain.shape[1]

    def out_copy(head):
        cols = pl.ds(head * width, width)
        return pltpu.make_async_copy(done_ref.at[:, cols], out_ref.at[:, cols], sem.at[head])

    group = len(parts) // groups
    for at in range(0, len(parts), group):
        for part in parts[at : at + group]:
            total, mix = states(part)
            square = jnp.mean(mix * mix, axis=1, keepdims=True)
            strength = lax.rsqrt(square + 1e-06 * (total * total))
            normed = (mix * strength * gain).astype(NARROW)
            for start in range(0, part.size, length):
                head = (part.start + start) // length
                done_ref[:, pl.ds(head * width, width)] = normed[start : start + length]
        first = parts[at].start // length
        for head in range(first, first + group * parts[at].size // length):
            out_copy(head).start()
    for head in range(out_ref.shape[1] // width):
        out_copy(head).wait()


def update(moved_ref, olds, news, keys, values, limits):
    for part in pieces(moved_ref.shape[0], NEAR_PIECES):
        fresh = take_in(
            moved_ref[part, :], keys, values, limits, *(old[part, :] for old in olds)
        )
        for new, value in zip(news, fresh):
            new[part, :] = value


def ready(pack_ref, mate_ref, ready_ref):
    width = pack_ref.shape[0]
    length = pack_ref.shape[1] - 2 * width
    keys = pack_ref[:, :length]
    through = dot(mate_ref[:, pl.ds(length, width)], keys).astype(NARROW)
    ready_ref[:, :length] = jnp.where(lax.axis_index("seq") % 2 == 0, through, keys)
    ready_ref[:, length:] = pack_ref[:, length + width :]


def attend_near(
    moved_ref, peak_ref, sum_ref, mix_ref, small_ref, mate_ref, straight_ref, crossed_ref,
    peak_out, sum_out, mix_out, travel_out, out_ref, keys_ref, values_ref, done_ref, sem,
):
    length = out_ref.shape[0]
    place = lax.axis_index("seq")
    core, chip_place = place % 2, place // 2
    olds, news = (peak_ref, sum_ref, mix_ref), (peak_out, sum_out, mix_out)

    @pl.when(chip_place > 0)
    def _():
        order = [mate_ref] + pairs_of([straight_ref, crossed_ref])
        travel_out[...] = gather(order, core, keys_ref, values_ref, None, length)
        limits = ((1 - core) * length, 3 * length)
        update(moved_ref, olds, news, keys_ref[...], values_ref[...], limits)

    @pl.when((chip_place == 0) & (core == 1))
    def _():
        span = pl.ds(0, length)
        gather([mate_ref], core, keys_ref, values_ref, None, length)
        update(moved_ref, olds, news, keys_ref[:, span], values_ref[span, :], None)

    @pl.when((chip_place == 0) & (core == 0))
    def _():
        parts = pieces(moved_ref.shape[0], SETTLE_PIECES)
        states = lambda part: (sum_out[part, :], mix_out[part, :])
        settle(out_ref, done_ref, sem, small_ref[small_ref.shape[0] - 1 :, :], parts, SETTLE_GROUPS, states)


def attend_next(
    moved_ref, peak_ref, sum_ref, mix_ref, travel_ref, out_in, small_ref, straight_ref, crossed_ref,
    peak_out, sum_out, mix_out, travel_out, out_ref, keys_ref, values_ref, done_ref, sem,
):
    length = out_ref.shape[0]
    place = lax.axis_index("seq")
    chip_place = place // 2
    olds, news = (peak_ref, sum_ref, mix_ref), (peak_out, sum_out, mix_out)

    @pl.when(chip_place > 1)
    def _():
        order = pairs_of([straight_ref, crossed_ref])
        travel_out[...] = gather(order, place % 2, keys_ref, values_ref, travel_ref[...], length)
        update(moved_ref, olds, news, keys_ref[...], values_ref[...], None)

    @pl.when((place > 0) & (chip_place <= 2))
    def _():
        parts = pieces(moved_ref.shape[0], SETTLE_PIECES)
        states = lambda part: (sum_out[part, :], mix_out[part, :])
        settle(out_ref, done_ref, sem, small_ref[small_ref.shape[0] - 1 :, :], parts, SETTLE_GROUPS, states)


def attend_last(*refs):
    moved_ref, peak_ref, sum_ref, mix_ref, travel_ref, _, small_ref = refs[:7]
    out_ref, keys_ref, values_ref, done_ref, sem = refs[-5:]
    far = refs[7:-5]
    length = out_ref.shape[0]
    place = lax.axis_index("seq")
    core, chip_place = place % 2, place // 2

    @pl.when(chip_place > 2)
    def _():
        order = pairs_of(far[:-2])
        travel = gather(order, core, keys_ref, values_ref, travel_ref[...], length)
        straight, crossed = far[-2][...], far[-1][...]
        pair = [jnp.where(core == 1, straight, crossed), jnp.where(core == 1, crossed, straight)]
        keys = jnp.concatenate([block[:, :length] for block in pair], axis=1)
        keys = dot(jnp.concatenate(halves(travel), axis=1), jnp.concatenate([keys, keys], axis=0))
        keys_ref[:, pl.ds(len(order) * length, 2 * length)] = keys.astype(NARROW)
        for slot, block in enumerate(pair, len(order)):
            values_ref[pl.ds(slot * length, length), :] = counted(block[:, length:])
        limits = (0, 2 * (chip_place - 2) * length) if order else None
        parts = pieces(moved_ref.shape[0], LAST_PIECES)
        states = lambda part: take_in(
            moved_ref[part, :], keys_ref[...], values_ref[...], limits,
            peak_ref[part, :], sum_ref[part, :], mix_ref[part, :],
        )[1:]
        settle(out_ref, done_ref, sem, small_ref[small_ref.shape[0] - 1 :, :], parts, LAST_GROUPS, states)


LOCAL = pl.BlockSpec(memory_space=pltpu.VMEM)
ANYWHERE = pl.BlockSpec(memory_space=pltpu.HBM)


def call(kernel, outs, count, scratch=(), flops=1e8, spots=None, aliases=None, places=None):
    return pl.pallas_call(
        kernel,
        out_shape=outs,
        in_specs=places or [LOCAL] * count,
        out_specs=spots or jax.tree.map(lambda _: LOCAL, outs),
        scratch_shapes=list(scratch),
        input_output_aliases=aliases or {},
        compiler_params=pltpu.CompilerParams(vmem_limit_bytes=16 << 20),
        cost_estimate=pl.CostEstimate(
            flops=int(flops), bytes_accessed=1 << 20, transcendentals=1 << 17
        ),
    )


def shards(queries, keys, values, directions, beta, gain):
    length, half = directions.shape
    width = 2 * half
    heads = queries.shape[1] // width
    segments = lax.axis_size("seq")
    places = range(lax.axis_size("head"))

    def partner(block):
        return lax.ppermute(block, "head", [(place, place ^ 1) for place in places])

    other_dirs = partner(directions.T)
    own = jnp.concatenate([keys.T, values.T], axis=0)
    other = partner(own)
    shape = jax.ShapeDtypeStruct
    small = jnp.concatenate([beta.T, gain.reshape(1, -1)], axis=0)
    square = shape((width, length), NARROW)
    inverse, dirs_t, dirs, coef, spread, transform = call(
        invert,
        (
            shape((2, length, length), NARROW),
            square,
            square,
            shape((8, length), WIDE),
            shape((2, length, width), NARROW),
            shape((width, width), NARROW),
        ),
        3,
        [pltpu.VMEM((width, length), NARROW)],
    )(directions.T, other_dirs, small)
    pack, solved, sides = call(
        prepare,
        (
            shape((width, 2 * length + width), NARROW),
            shape((2, length, length + width), NARROW),
            shape((width, 2 * length), NARROW),
        ),
        8,
        [pltpu.VMEM((2, width, length), NARROW)],
    )(own, other, inverse, dirs_t, dirs, coef, spread, transform)

    def across(block):
        return lax.ppermute(block, "seq", [(i, i ^ 1) for i in range(segments)])

    mate = across(pack)
    chips = segments // 2
    far = []
    for chip in range(1, chips):
        pairs = [(i, (i + 2 * chip) % segments) for i in range(segments)]
        block = pack
        if chip == chips - 1:
            block = call(ready, shape((width, length + width), NARROW), 2)(pack, mate)
        far.append(lax.ppermute(block, "seq", pairs))
    state_shape = (shape((heads * length, width), WIDE),) * 3
    moved, *state = call(
        own_segment, (shape((heads * length, width), NARROW),) + state_shape, 5
    )(queries, solved, sides, coef, pack)

    def stores(count):
        return [
            pltpu.VMEM((width, count * length), NARROW),
            pltpu.VMEM((count * length, 2 * width), NARROW),
        ]

    crossed = across(far[0])
    states = state_shape + (shape((width, width), WIDE), shape((length, heads * width), NARROW))
    spots = (LOCAL,) * 4 + (ANYWHERE,)
    ends = [pltpu.VMEM((length, heads * width), NARROW), pltpu.SemaphoreType.DMA((heads,))]
    in_place = {1: 0, 2: 1, 3: 2}
    *state, travel, out = call(
        attend_near, states, 8, stores(3) + ends, spots=spots, aliases=in_place
    )(moved, *state, small, mate, far[0], crossed)
    places = [ANYWHERE if at == 5 else LOCAL for at in range(9)]
    crossed = across(far[1])
    *state, travel, out = call(
        attend_next,
        states,
        9,
        stores(2) + ends,
        spots=spots,
        aliases={**in_place, 4: 3, 5: 4},
        places=places,
    )(moved, *state, travel, out, small, far[1], crossed)
    blocks = []
    for chip in range(3, chips):
        blocks += [far[chip - 1], across(far[chip - 1])]
    count = 7 + len(blocks)
    return call(
        attend_last,
        shape((length, heads * width), NARROW),
        count,
        stores(2 * (chips - 3)) + ends,
        flops=1e9,
        spots=ANYWHERE,
        aliases={5: 0},
        places=[ANYWHERE if at == 5 else LOCAL for at in range(count)],
    )(moved, *state, travel, out, small, *blocks)


def solution(mesh):
    placed = (
        P("seq", "head"),
        P("seq", "head"),
        P("seq", "head"),
        P("seq", "head"),
        P("seq", None),
        P(),
    )

    return jax.shard_map(
        shards, mesh=mesh, in_specs=placed, out_specs=P("seq", "head"), check_vma=False
    )
```

```python
import math

import jax
import jax.numpy as jnp
from jax import lax
from jax.experimental import pallas as pl
from jax.experimental.pallas import tpu as pltpu
from jax.sharding import PartitionSpec as P


WIDE = jnp.float32
NARROW = jnp.bfloat16
MASKED = -1e30
LAST_PIECES, LAST_GROUPS = 8, 4
SETTLE_PIECES, SETTLE_GROUPS = 8, 4
OWN_PIECES, NEAR_PIECES = 1, 2


def halves(x):
    top = x.astype(NARROW)
    return top, (x - top.astype(WIDE)).astype(NARROW)


def dot(a, b):
    return jnp.dot(a, b, preferred_element_type=WIDE)


def dot3(a, b):
    a_top, a_low = a
    b_top, b_low = b
    return dot(
        jnp.concatenate([a_top, a_low, a_top], axis=1),
        jnp.concatenate([b_top, b_top, b_low], axis=0),
    )


def whole(full_ref, own, other, parity):
    half = own.shape[0]
    full_ref[pl.ds(parity * half, half), :] = own
    full_ref[pl.ds((1 - parity) * half, half), :] = other
    return full_ref[...]


def invert(own_ref, other_ref, small_ref, inverse_ref, across_ref, dirs_ref, coef_ref, full_ref):
    length = own_ref.shape[1]
    place = lax.axis_index("head")
    parity = place % 2
    dirs_t = whole(full_ref, own_ref[...], other_ref[...], parity)
    across_ref[...] = dirs_t
    dirs_wide = dirs_t.astype(WIDE)
    dirs = dirs_wide.T.astype(NARROW)
    dirs_ref[...] = dirs
    power = jnp.sum(dirs_wide * dirs_wide, axis=0, keepdims=True) + 1e-06
    coef = small_ref[pl.ds(place // 2, 1), :] / power
    coef_ref[...] = jnp.broadcast_to(coef, coef_ref.shape)

    row = lax.broadcasted_iota(jnp.int32, (length, length), 0)
    col = lax.broadcasted_iota(jnp.int32, (length, length), 1)
    below = jnp.where(row > col, dot(dirs, dirs_t) * coef, 0.0)

    pair = jnp.where((row ^ col) == 1, -below, 0.0)
    joint = jnp.where((row // 2) ^ (col // 2) == 1, below, 0.0)
    joint = joint + jnp.sum(pair, axis=1, keepdims=True) * pltpu.roll(joint, 1, 0)
    joint = joint + pltpu.roll(joint, length - 1, 1) * jnp.sum(pair, axis=0, keepdims=True)
    inverse = jnp.where(row == col, 1.0, 0.0) + pair - joint
    block = 4
    while block < length:
        joint = halves(jnp.where((row // block) ^ (col // block) == 1, below, 0.0))
        parts = halves(inverse)
        step = block if block % 8 == 0 else length
        starts = range(step % length, length, 2 * step)
        lower = [jnp.concatenate([p[s : s + step] for s in starts], axis=0) for p in parts]
        change = dot3(halves(dot3(lower, joint)), parts)
        if step == length:
            inverse = inverse - change
        else:
            rows = []
            for at, start in enumerate(starts):
                rows.append(inverse[start - step : start])
                rows.append(inverse[start : start + step] - change[at * step : (at + 1) * step])
            inverse = jnp.concatenate(rows, axis=0)
        block *= 2
    inverse_ref[0], inverse_ref[1] = halves(inverse)


def prepare(
    own_ref, other_ref, inverse_ref, across_ref, dirs_ref, coef_ref,
    pack_ref, solved_ref, sides_ref, full_ref,
):
    half, length = own_ref.shape[0] // 2, own_ref.shape[1]
    width = 2 * half
    parity = lax.axis_index("head") % 2
    keys_t = whole(full_ref.at[0], own_ref[:half, :], other_ref[:half, :], parity)
    values_t = whole(full_ref.at[1], own_ref[half:, :], other_ref[half:, :], parity)
    dirs_t, dirs = across_ref[...], dirs_ref[...]
    row = lax.broadcasted_iota(jnp.int32, (length, length), 0)
    col = lax.broadcasted_iota(jnp.int32, (length, length), 1)
    top, low = inverse_ref[0], inverse_ref[1]
    reach_top, reach_low = halves(jnp.where(row > col, dot(dirs, keys_t), 0.0))
    right = jnp.concatenate([reach_top, dirs], axis=1)
    solved = dot(jnp.concatenate([top, low], axis=1), jnp.concatenate([right, right], axis=0))
    solved_reach = solved[:, :length] + dot(top, reach_low)
    solved_parts = halves(jnp.concatenate([solved_reach, solved[:, length:]], axis=1))
    change = dot3(halves(dirs_t.astype(WIDE) * coef_ref[:1, :]), solved_parts)
    pack_ref[:, :length] = (keys_t.astype(WIDE) - change[:, :length]).astype(NARROW)
    row_w = lax.broadcasted_iota(jnp.int32, (width, width), 0)
    col_w = lax.broadcasted_iota(jnp.int32, (width, width), 1)
    unit = jnp.where(row_w == col_w, 1.0, 0.0)
    pack_ref[:, length : length + width] = (unit - change[:, length:]).astype(NARROW)
    pack_ref[:, length + width :] = values_t.astype(WIDE).T.astype(NARROW)
    solved_ref[0] = solved_parts[0]
    solved_ref[1] = solved_parts[1]
    sides_ref[...] = jnp.concatenate([dirs_t, keys_t], axis=1)


def own_segment(
    queries_ref, solved_ref, sides_ref, coef_ref, pack_ref, moved_ref, peak_ref, sum_ref, mix_ref
):
    length = queries_ref.shape[0]
    width = sides_ref.shape[0]
    top, low = solved_ref[0], solved_ref[1]
    right = jnp.concatenate([top, top, low], axis=0)
    values = counted(pack_ref[:, length + width :])
    for part in pieces(moved_ref.shape[0], OWN_PIECES):
        heads = range(part.start // length, (part.start + part.size) // length)
        query = jnp.concatenate([queries_ref[:, pl.ds(h * width, width)] for h in heads], axis=0)
        row = lax.broadcasted_iota(jnp.int32, (part.size, length), 0) % length
        col = lax.broadcasted_iota(jnp.int32, (part.size, length), 1)
        past = row >= col
        plain = dot(query, sides_ref[...])
        met_top, met_low = halves(jnp.where(past, plain[:, :length] * coef_ref[:1, :], 0.0))
        change = dot(jnp.concatenate([met_top, met_low, met_top], axis=1), right)
        moved_ref[part, :] = (query.astype(WIDE) - change[:, length:]).astype(NARROW)
        scores = jnp.where(past, plain[:, length:] - change[:, :length], MASKED)
        peak = jnp.max(scores, axis=1, keepdims=True)
        mixed = dot(powers(scores, peak, width).astype(NARROW), values)
        peak_ref[part, :] = jnp.broadcast_to(peak, (part.size, width))
        mix_ref[part, :] = mixed[:, :width]
        sum_ref[part, :] = mixed[:, width:]


def counted(values):
    return jnp.concatenate([values, jnp.ones_like(values)], axis=1)


def powers(scores, peak, width):
    return jnp.exp2((scores - peak) * (width ** (-0.5) * math.log2(math.e)))


def carry(travel, block, length):
    both = dot(jnp.concatenate(halves(travel), axis=1), jnp.concatenate([block, block], axis=0))
    return both[:, :length].astype(NARROW), both[:, length:]


def gather(refs, core, keys_ref, values_ref, travel, length):
    width = keys_ref.shape[0]
    for slot, ref in enumerate(refs):
        if isinstance(ref, tuple):
            block = jnp.where(core == 1, ref[0][...], ref[1][...])
        else:
            block = ref[...]
        at = pl.ds(slot * length, length)
        values_ref[at, :] = counted(block[:, length + width :])
        block = block[:, : length + width]
        if travel is None:
            keys_ref[:, at] = block[:, :length]
            row = lax.broadcasted_iota(jnp.int32, (width, width), 0)
            col = lax.broadcasted_iota(jnp.int32, (width, width), 1)
            unit = jnp.where(row == col, 1.0, 0.0)
            travel = jnp.where(core == 1, block[:, length:].astype(WIDE), unit)
        else:
            keys_ref[:, at], travel = carry(travel, block, length)
    return travel


def pairs_of(far):
    order = []
    for straight, crossed in zip(far[::2], far[1::2]):
        order += [(straight, crossed), (crossed, straight)]
    return order


def take_in(query, keys, values, limits, peak, total, mix):
    width = mix.shape[1]
    scores = dot(query, keys)
    if limits is not None:
        column = lax.broadcasted_iota(jnp.int32, scores.shape, 1)
        scores = jnp.where((column >= limits[0]) & (column < limits[1]), scores, MASKED)
    above = jnp.maximum(peak, jnp.max(scores, axis=1, keepdims=True))
    fade = powers(peak, above, width)
    level = jnp.concatenate([above] * (scores.shape[1] // width), axis=1)
    mixed = dot(powers(scores, level, width).astype(NARROW), values)
    return above, total * fade + mixed[:, width:], mix * fade + mixed[:, :width]


def pieces(rows, count):
    size = rows // count
    return [pl.ds(start, size) for start in range(0, rows, size)]


def settle(out_ref, done_ref, sem, gain, parts, groups, states):
    length, width = out_ref.shape[0], gain.shape[1]

    def out_copy(head):
        cols = pl.ds(head * width, width)
        return pltpu.make_async_copy(done_ref.at[:, cols], out_ref.at[:, cols], sem.at[head])

    group = len(parts) // groups
    for at in range(0, len(parts), group):
        for part in parts[at : at + group]:
            total, mix = states(part)
            square = jnp.mean(mix * mix, axis=1, keepdims=True)
            strength = lax.rsqrt(square + 1e-06 * (total * total))
            normed = (mix * strength * gain).astype(NARROW)
            for start in range(0, part.size, length):
                head = (part.start + start) // length
                done_ref[:, pl.ds(head * width, width)] = normed[start : start + length]
        first = parts[at].start // length
        for head in range(first, first + group * parts[at].size // length):
            out_copy(head).start()
    for head in range(out_ref.shape[1] // width):
        out_copy(head).wait()


def update(moved_ref, olds, news, keys, values, limits):
    for part in pieces(moved_ref.shape[0], NEAR_PIECES):
        fresh = take_in(
            moved_ref[part, :], keys, values, limits, *(old[part, :] for old in olds)
        )
        for new, value in zip(news, fresh):
            new[part, :] = value


def ready(pack_ref, mate_ref, ready_ref):
    width = pack_ref.shape[0]
    length = pack_ref.shape[1] - 2 * width
    keys = pack_ref[:, :length]
    through = dot(mate_ref[:, pl.ds(length, width)], keys).astype(NARROW)
    ready_ref[:, :length] = jnp.where(lax.axis_index("seq") % 2 == 0, through, keys)
    ready_ref[:, length:] = pack_ref[:, length + width :]


def attend_near(
    moved_ref, peak_ref, sum_ref, mix_ref, small_ref, mate_ref, straight_ref, crossed_ref,
    peak_out, sum_out, mix_out, travel_out, out_ref, keys_ref, values_ref, done_ref, sem,
):
    length = out_ref.shape[0]
    place = lax.axis_index("seq")
    core, chip_place = place % 2, place // 2
    olds, news = (peak_ref, sum_ref, mix_ref), (peak_out, sum_out, mix_out)

    @pl.when(chip_place > 0)
    def _():
        order = [mate_ref] + pairs_of([straight_ref, crossed_ref])
        travel_out[...] = gather(order, core, keys_ref, values_ref, None, length)
        limits = ((1 - core) * length, 3 * length)
        update(moved_ref, olds, news, keys_ref[...], values_ref[...], limits)

    @pl.when((chip_place == 0) & (core == 1))
    def _():
        span = pl.ds(0, length)
        gather([mate_ref], core, keys_ref, values_ref, None, length)
        update(moved_ref, olds, news, keys_ref[:, span], values_ref[span, :], None)

    @pl.when((chip_place == 0) & (core == 0))
    def _():
        parts = pieces(moved_ref.shape[0], SETTLE_PIECES)
        states = lambda part: (sum_out[part, :], mix_out[part, :])
        settle(out_ref, done_ref, sem, small_ref[small_ref.shape[0] - 1 :, :], parts, SETTLE_GROUPS, states)


def attend_next(
    moved_ref, peak_ref, sum_ref, mix_ref, travel_ref, out_in, small_ref, straight_ref, crossed_ref,
    peak_out, sum_out, mix_out, travel_out, out_ref, keys_ref, values_ref, done_ref, sem,
):
    length = out_ref.shape[0]
    place = lax.axis_index("seq")
    chip_place = place // 2
    olds, news = (peak_ref, sum_ref, mix_ref), (peak_out, sum_out, mix_out)

    @pl.when(chip_place > 1)
    def _():
        order = pairs_of([straight_ref, crossed_ref])
        travel_out[...] = gather(order, place % 2, keys_ref, values_ref, travel_ref[...], length)
        update(moved_ref, olds, news, keys_ref[...], values_ref[...], None)

    @pl.when((place > 0) & (chip_place <= 2))
    def _():
        parts = pieces(moved_ref.shape[0], SETTLE_PIECES)
        states = lambda part: (sum_out[part, :], mix_out[part, :])
        settle(out_ref, done_ref, sem, small_ref[small_ref.shape[0] - 1 :, :], parts, SETTLE_GROUPS, states)


def attend_last(*refs):
    moved_ref, peak_ref, sum_ref, mix_ref, travel_ref, _, small_ref = refs[:7]
    out_ref, keys_ref, values_ref, done_ref, sem = refs[-5:]
    far = refs[7:-5]
    length = out_ref.shape[0]
    place = lax.axis_index("seq")
    core, chip_place = place % 2, place // 2

    @pl.when(chip_place > 2)
    def _():
        order = pairs_of(far[:-2])
        travel = gather(order, core, keys_ref, values_ref, travel_ref[...], length)
        straight, crossed = far[-2][...], far[-1][...]
        pair = [jnp.where(core == 1, straight, crossed), jnp.where(core == 1, crossed, straight)]
        keys = jnp.concatenate([block[:, :length] for block in pair], axis=1)
        keys = dot(jnp.concatenate(halves(travel), axis=1), jnp.concatenate([keys, keys], axis=0))
        keys_ref[:, pl.ds(len(order) * length, 2 * length)] = keys.astype(NARROW)
        for slot, block in enumerate(pair, len(order)):
            values_ref[pl.ds(slot * length, length), :] = counted(block[:, length:])
        limits = (0, 2 * (chip_place - 2) * length) if order else None
        parts = pieces(moved_ref.shape[0], LAST_PIECES)
        states = lambda part: take_in(
            moved_ref[part, :], keys_ref[...], values_ref[...], limits,
            peak_ref[part, :], sum_ref[part, :], mix_ref[part, :],
        )[1:]
        settle(out_ref, done_ref, sem, small_ref[small_ref.shape[0] - 1 :, :], parts, LAST_GROUPS, states)


LOCAL = pl.BlockSpec(memory_space=pltpu.VMEM)
ANYWHERE = pl.BlockSpec(memory_space=pltpu.HBM)


def call(kernel, outs, count, scratch=(), flops=1e8, spots=None, aliases=None, places=None):
    return pl.pallas_call(
        kernel,
        out_shape=outs,
        in_specs=places or [LOCAL] * count,
        out_specs=spots or jax.tree.map(lambda _: LOCAL, outs),
        scratch_shapes=list(scratch),
        input_output_aliases=aliases or {},
        compiler_params=pltpu.CompilerParams(vmem_limit_bytes=16 << 20),
        cost_estimate=pl.CostEstimate(
            flops=int(flops), bytes_accessed=1 << 20, transcendentals=1 << 17
        ),
    )


def shards(queries, keys, values, directions, beta, gain):
    length, half = directions.shape
    width = 2 * half
    heads = queries.shape[1] // width
    segments = lax.axis_size("seq")
    places = range(lax.axis_size("head"))

    def partner(block):
        return lax.ppermute(block, "head", [(place, place ^ 1) for place in places])

    other_dirs = partner(directions.T)
    own = jnp.concatenate([keys.T, values.T], axis=0)
    other = partner(own)
    shape = jax.ShapeDtypeStruct
    small = jnp.concatenate([beta.T, gain.reshape(1, -1)], axis=0)
    square = shape((width, length), NARROW)
    inverse, dirs_t, dirs, coef = call(
        invert,
        (shape((2, length, length), NARROW), square, square, shape((8, length), WIDE)),
        3,
        [pltpu.VMEM((width, length), NARROW)],
    )(directions.T, other_dirs, small)
    pack, solved, sides = call(
        prepare,
        (
            shape((width, 2 * length + width), NARROW),
            shape((2, length, length + width), NARROW),
            shape((width, 2 * length), NARROW),
        ),
        6,
        [pltpu.VMEM((2, width, length), NARROW)],
    )(own, other, inverse, dirs_t, dirs, coef)

    def across(block):
        return lax.ppermute(block, "seq", [(i, i ^ 1) for i in range(segments)])

    mate = across(pack)
    chips = segments // 2
    far = []
    for chip in range(1, chips):
        pairs = [(i, (i + 2 * chip) % segments) for i in range(segments)]
        block = pack
        if chip == chips - 1:
            block = call(ready, shape((width, length + width), NARROW), 2)(pack, mate)
        far.append(lax.ppermute(block, "seq", pairs))
    state_shape = (shape((heads * length, width), WIDE),) * 3
    moved, *state = call(
        own_segment, (shape((heads * length, width), NARROW),) + state_shape, 5
    )(queries, solved, sides, coef, pack)

    def stores(count):
        return [
            pltpu.VMEM((width, count * length), NARROW),
            pltpu.VMEM((count * length, 2 * width), NARROW),
        ]

    crossed = across(far[0])
    states = state_shape + (shape((width, width), WIDE), shape((length, heads * width), NARROW))
    spots = (LOCAL,) * 4 + (ANYWHERE,)
    ends = [pltpu.VMEM((length, heads * width), NARROW), pltpu.SemaphoreType.DMA((heads,))]
    in_place = {1: 0, 2: 1, 3: 2}
    *state, travel, out = call(
        attend_near, states, 8, stores(3) + ends, spots=spots, aliases=in_place
    )(moved, *state, small, mate, far[0], crossed)
    places = [ANYWHERE if at == 5 else LOCAL for at in range(9)]
    crossed = across(far[1])
    *state, travel, out = call(
        attend_next,
        states,
        9,
        stores(2) + ends,
        spots=spots,
        aliases={**in_place, 4: 3, 5: 4},
        places=places,
    )(moved, *state, travel, out, small, far[1], crossed)
    blocks = []
    for chip in range(3, chips):
        blocks += [far[chip - 1], across(far[chip - 1])]
    count = 7 + len(blocks)
    return call(
        attend_last,
        shape((length, heads * width), NARROW),
        count,
        stores(2 * (chips - 3)) + ends,
        flops=1e9,
        spots=ANYWHERE,
        aliases={5: 0},
        places=[ANYWHERE if at == 5 else LOCAL for at in range(count)],
    )(moved, *state, travel, out, small, *blocks)


def solution(mesh):
    placed = (
        P("seq", "head"),
        P("seq", "head"),
        P("seq", "head"),
        P("seq", "head"),
        P("seq", None),
        P(),
    )

    return jax.shard_map(
        shards, mesh=mesh, in_specs=placed, out_specs=P("seq", "head"), check_vma=False
    )
```
